1024 devices in a mesh: gx: 16 (over z_lo), gy: 8 (over z_hi, y), gz: 8 (over x, core).
Axes of the slice: x: 4, y: 4, z: 32 (z_hi: 2, z_lo: 16; z = z_hi * 16 + z_lo), core: 2. Of those that a mesh axis runs over, the one named last changes fastest.
Arguments:
- state: float32 [9, 256, 128, 1024], P(None, 'gx', 'gy', 'gz'), may hold values from 0 to 1
- mobility: float32 [8], replicated, may hold values from 0.5 to 2
- seeds: int32 [2, 2, 256, 128], replicated, may hold values from 0 to 8
- frame_shifts: int32 [2], replicated, may hold values from 0 to 2, as said below
Outputs:
- state_out: float32 [9, 256, 128, 1024], P(None, 'gx', 'gy', 'gz')
The draws below stay inside these ranges and needn't reach their ends.
Inputs may be any that keep to these rules, and one draw needn't show every extreme that they name: A value of 8 seeds no grain in that cell. `frame_shifts`: the frame advances 2 planes in at least one step and stays in place in at least one other.
All inputs are finite; a program needn't handle non-finite values.
Results may differ from the reference program's by a relative error of at most 0.0001.
Values sent between devices are 32-bit elements; how exact they have to be, the bound alone decides.
A program may use at most 32 MiB of HBM per device.

```python
import math
import jax
import jax.numpy as jnp
from jax import lax

GRAINS = 8
STEPS = 2
SHIFT_MAX = 2
NX = 256
NY = 128
NZ = 1024


def draw_frame_shifts(key, part):
    counts = jax.random.randint(key, (STEPS,), 0, SHIFT_MAX + 1, dtype=jnp.int32)
    which = jax.random.randint(jax.random.fold_in(key, 7), (), 0, STEPS, dtype=jnp.int32)
    offset = jax.random.randint(jax.random.fold_in(key, 11), (), 0, STEPS - 1, dtype=jnp.int32)
    other = (which + 1 + offset) % STEPS
    steps_all = jnp.arange(STEPS, dtype=jnp.int32)
    counts = jnp.where(steps_all == other, 0, counts)
    return jnp.where(steps_all == which, SHIFT_MAX, counts).astype(jnp.int32)


def plant(array, stream_key, least, largest):
    longest = array.shape.index(max(array.shape))
    spots = []
    for shift in (0, 1):
        where = [jax.random.randint(jax.random.fold_in(stream_key, axis), (), 0, length) for axis, length in enumerate(array.shape)]
        where[longest] = (where[longest] + shift) % array.shape[longest]
        spots.append(tuple(where))
    return array.at[spots[0]].set(least).at[spots[1]].set(largest)


def level_of(own_key, dims, cuts, smallest, top_value):
    loudness = 1.0
    for dim, parts in cuts:
        draws = jax.random.uniform(jax.random.fold_in(jax.random.fold_in(own_key, 6), dim), (parts,), jnp.float32, smallest / len(cuts), top_value / len(cuts))
        loudness = loudness * jnp.repeat(jnp.exp(draws), dims[dim] // parts).reshape((-1,) + (1,) * (len(dims) - 1 - dim))
    return loudness


def setup_inputs(seed: int = 0) -> dict:
    keys = jax.random.split(jax.random.key(seed), 5)
    state = jnp.clip(1.0 * jax.random.uniform(keys[0], (GRAINS + 1, NX, NY, NZ), jnp.float32) ** level_of(keys[0], (GRAINS + 1, NX, NY, NZ), ((1, 16), (2, 8), (3, 8)), -0.2, 0.2), 0.0, 1.0)
    mobility = jnp.clip(jnp.exp(jax.random.uniform(keys[1], (GRAINS,), jnp.float32, math.log(0.5), math.log(2.0))), 0.5, 2.0)
    seeds = plant(jax.random.randint(keys[2], (STEPS, SHIFT_MAX, NX, NY), 0, GRAINS + 1), jax.random.fold_in(keys[2], 1), 0, GRAINS).astype(jnp.int32)
    frame_shifts = draw_frame_shifts(jax.random.fold_in(keys[4], 71), 0)
    return dict(state=state, mobility=mobility, seeds=seeds, frame_shifts=frame_shifts)


step_rate = 0.1
stiffness = 0.7
coupling = 0.5
diffusion = 0.14
rejection = 0.5
nucleus = 0.3
melt_solute = 1.0


def laplace(field):
    padded = jnp.pad(field, ((1, 1), (1, 1), (0, 0)), mode="wrap")
    padded = jnp.pad(padded, ((0, 0), (0, 0), (1, 1)))
    center = padded[1:-1, 1:-1, 1:-1]
    beside = padded[:-2, 1:-1, 1:-1] + padded[2:, 1:-1, 1:-1] + padded[1:-1, :-2, 1:-1] + padded[1:-1, 2:, 1:-1]
    beside = beside + padded[1:-1, 1:-1, :-2] + padded[1:-1, 1:-1, 2:]
    return beside - 6.0 * center


def advance(moved, mobility):
    phases = moved[:GRAINS]
    solute = moved[GRAINS]
    squares = jnp.sum(phases * phases, axis=0)
    zpos = jnp.arange(NZ, dtype=jnp.float32)
    theta = 1.0 - 2.0 * (zpos + 0.5) / NZ
    alpha = theta - coupling * solute

    def single(item):
        phase, speed = item
        drive = -alpha * phase + phase * phase * phase + phase * (squares - phase * phase)
        return phase + step_rate * speed * (stiffness * laplace(phase) - drive)

    fresh = lax.map(single, (phases, mobility))
    squares_new = jnp.sum(fresh * fresh, axis=0)
    solute_new = solute + diffusion * laplace(solute) - rejection * solute * (squares_new - squares)
    return jnp.concatenate([fresh, solute_new[None]], axis=0)


def reference(state, mobility, seeds, frame_shifts):
    field = state
    grains = jnp.arange(GRAINS, dtype=jnp.int32)
    for step in range(STEPS):
        count = frame_shifts[step].astype(jnp.int32)
        marks = jnp.transpose(seeds[step], (1, 2, 0))
        nuclei = nucleus * (marks[None] == grains[:, None, None, None]).astype(jnp.float32)
        melt = jnp.full((1, NX, NY, SHIFT_MAX), melt_solute, jnp.float32)
        entering = jnp.concatenate([nuclei, melt], axis=0)
        moved = lax.dynamic_slice_in_dim(jnp.concatenate([field, entering], axis=3), count, NZ, axis=3)
        field = advance(moved, mobility)
    return field
```

```python
import functools

import jax
import jax.numpy as jnp
from jax import lax
from jax.experimental import pallas as pl
from jax.experimental.pallas import tpu as pltpu
from jax.sharding import PartitionSpec as P

step_rate = 0.1
stiffness = 0.7
coupling = 0.5
diffusion = 0.14
rejection = 0.5
nucleus = 0.3
melt_solute = 1.0

MESH = pl.DeviceIdType.MESH
FIELDS = 9
GRAINS = 8
W = 16
COLUMN = 4
f32 = jnp.float32


def iota(shape, dim):
    return lax.broadcasted_iota(jnp.int32, shape, dim)


def kernel(sizes, mob, shifts, state, seeds, out, F0, F1, H0, H1, relay, pack, packed, xl, xr, xlh, xrh, eh,
           E0m, E0h, E1m, E1h, E2m, marks, seedbuf, local, send, recv):
    nx, ny, nz = sizes
    gx, gy, gz = lax.axis_index("gx"), lax.axis_index("gy"), lax.axis_index("gz")
    col = lax.rem(gy, COLUMN)

    def at(dx, dy, dz=0):
        return (lax.rem(gx + dx + nx, nx), lax.rem(gy + dy + ny, ny), lax.rem(gz + dz + nz, nz))

    far = at(0, jnp.where(col >= 2, 2, -2))
    around = [at(1, 0), at(-1, 0), at(0, 1), at(0, -1), at(1, 1), at(1, -1), at(-1, 1), at(-1, -1)]
    partners = around + [at(0, 0, 1), at(0, 0, -1), far]

    barrier = pltpu.get_barrier_semaphore()
    for partner in partners:
        pl.semaphore_signal(barrier, inc=1, device_id=partner, device_id_type=MESH)

    own = [
        pltpu.make_async_copy(state, F0.at[:, 2:18], local.at[0]),
        pltpu.make_async_copy(state.at[:, :, 0:1], H0.at[:, 2:18, 2:3], local.at[1]),
        pltpu.make_async_copy(state.at[:, :, 15:16], H0.at[:, 2:18, 4:5], local.at[2]),
        pltpu.make_async_copy(seeds, seedbuf, local.at[3]),
    ]
    for copy in own:
        copy.start()

    lane = iota((8, 128), 1)
    row = iota((8, 128), 0)
    group = lane // 6
    spot = lane - 6 * group

    own[0].wait()
    for f in range(FIELDS):
        for t in range(2):
            rows = slice(8 * t, 8 * t + 8)
            acc = jnp.zeros((8, 128), f32)
            for x in range(W):
                moved = pltpu.roll(F0[f, x + 2, rows], 6 * (x + 2) + 2, 1)
                acc = jnp.where((group == x + 2) & (spot >= 2), moved, acc)
            pack[f, rows] = acc
    for t in range(2):
        rows = slice(8 * t, 8 * t + 8)
        low = jnp.zeros((8, 128), f32)
        high = jnp.zeros((8, 128), f32)
        for f in range(FIELDS):
            acc = pack[f, rows]
            here = lane // 12 == f
            low = jnp.where(here, pltpu.roll(acc, (12 * f - 12) % 128, 1), low)
            high = jnp.where(here, pltpu.roll(acc, (12 * f - 96) % 128, 1), high)
        pack[FIELDS, rows] = low
        pack[FIELDS + 1, rows] = high

    pl.semaphore_wait(barrier, len(partners))

    def remote(src, dst, s, r, device):
        return pltpu.make_async_remote_copy(
            src_ref=src, dst_ref=dst, send_sem=send.at[s], recv_sem=recv.at[r], device_id=device, device_id_type=MESH
        )

    A, B = slice(0, 8), slice(8, 16)
    hA, hB = slice(2, 10), slice(10, 18)
    top, bottom = slice(14, 16), slice(0, 2)
    up_a = remote(state.at[:, A, top], H0.at[:, hA, 0:2], 0, 0, at(0, 1))
    up_b = remote(state.at[:, B, top], H0.at[:, hB, 0:2], 1, 1, at(0, 1))
    down_a = remote(state.at[:, A, bottom], H0.at[:, hA, 5:7], 2, 2, at(0, -1))
    down_b = remote(state.at[:, B, bottom], H0.at[:, hB, 5:7], 3, 3, at(0, -1))
    up_r = remote(state.at[:, B, top], relay, 1, 4, at(0, -1))
    down_r = remote(state.at[:, B, bottom], relay, 3, 4, at(0, 1))
    on_up = remote(relay, H0.at[:, hB, 0:2], 4, 1, far)
    on_down = remote(relay, H0.at[:, hB, 5:7], 4, 3, far)

    @pl.when(col == COLUMN - 1)
    def _():
        up_r.start()

    @pl.when(col == 0)
    def _():
        down_r.start()

    up_a.start()
    down_a.start()

    @pl.when(col != COLUMN - 1)
    def _():
        up_b.start()

    @pl.when(col != 0)
    def _():
        down_b.start()

    first = [
        remote(state.at[:, 14:16], F0.at[:, 0:2], 5, 5, at(1, 0)),
        remote(state.at[:, 0:2], F0.at[:, 18:20], 6, 6, at(-1, 0)),
        remote(state.at[:, 15:16, 15:16], H0.at[:, 1:2, 1:2], 7, 7, at(1, 1)),
        remote(state.at[:, 15:16, 0:1], H0.at[:, 1:2, 5:6], 8, 8, at(1, -1)),
        remote(state.at[:, 0:1, 15:16], H0.at[:, 18:19, 1:2], 9, 9, at(-1, 1)),
        remote(state.at[:, 0:1, 0:1], H0.at[:, 18:19, 5:6], 10, 10, at(-1, -1)),
    ]
    planes = remote(pack, packed, 11, 11, at(0, 0, -1))
    planes.start()
    for copy in first:
        copy.start()

    @pl.when(col == 2)
    def _():
        up_r.wait_recv()
        on_up.start()

    @pl.when(col == 1)
    def _():
        down_r.wait_recv()
        on_down.start()

    planes.wait_recv()
    second = [
        remote(packed.at[0:FIELDS, top], eh.at[:, 0:2], 12, 12, at(0, 1)),
        remote(packed.at[0:FIELDS, bottom], eh.at[:, 5:7], 13, 13, at(0, -1)),
        remote(packed.at[FIELDS + 1], xl, 14, 14, at(1, 0)),
        remote(packed.at[FIELDS], xr, 15, 15, at(-1, 0)),
        remote(packed.at[FIELDS + 1, 15:16], xlh.at[1:2], 16, 16, at(1, 1)),
        remote(packed.at[FIELDS + 1, 0:1], xlh.at[5:6], 17, 17, at(1, -1)),
        remote(packed.at[FIELDS, 15:16], xrh.at[1:2], 18, 18, at(-1, 1)),
        remote(packed.at[FIELDS, 0:1], xrh.at[5:6], 19, 19, at(-1, -1)),
    ]
    for copy in second:
        copy.start()

    own[3].wait()
    first_moves = jnp.full((8, 128), shifts[0], jnp.int32) == 2
    first_rows = jnp.full((256, 128), shifts[0], jnp.int32) == 2
    r24 = iota((24, 128), 0)
    offset = jnp.where(r24 < 16, r24, jnp.where(r24 <= 18, r24 - 18, r24 - 5))
    wanted = lax.rem(gy * W + offset + ny * W, ny * W)
    pick = (iota((24, 128), 1) == wanted).astype(f32)
    xrow = iota((256, 128), 0)
    wlane = iota((256, 128), 1)
    wgroup = wlane // 6
    wspot = wlane - 6 * wgroup
    same = lax.rem(gx * W - 2 + wgroup + nx * W, nx * W) == xrow
    total = jnp.zeros((24, 128), f32)
    for k in range(2):
        grid = jnp.where(first_rows, seedbuf[0, k], seedbuf[1, k]).astype(f32)
        lines = lax.dot_general(pick, grid, (((1,), (1,)), ((), ())), preferred_element_type=f32)
        spread = (same & (wspot == 2 + k)).astype(f32)
        total = total + jnp.dot(lines, spread, preferred_element_type=f32)
    marks[...] = total

    own[1].wait()
    own[2].wait()
    for copy in first:
        copy.wait()
    for copy in second:
        copy.wait()
    planes.wait_send()
    up_a.wait()
    down_a.wait()
    up_b.wait()
    down_b.wait()

    @pl.when((col == 1) | (col == 2))
    def _():
        on_up.wait_send()

    tiles = (slice(0, 8), slice(8, 16))
    last = jnp.full((8, 128), gz, jnp.int32) == nz - 1
    lowest = jnp.full((8, 128), gz, jnp.int32) == 0
    enters = (spot == 2) | (spot == 3)

    def gather_own(src, count, dst, base, lo, hi):
        def body(xi, carry):
            shift = lax.rem(6 * xi + 2, 128)
            mask = (group == xi) & (spot < 2)
            new = []
            for i in range(FIELDS * count):
                f, t = i // count, i % count
                moved = pltpu.roll(src[f, xi, 8 * t:8 * t + 8], shift, 1)
                new.append(jnp.where(mask, moved, carry[i]))
            return tuple(new)

        done = lax.fori_loop(lo, hi, body, tuple(base))
        for i in range(FIELDS * count):
            f, t = i // count, i % count
            dst[f, 8 * t:8 * t + 8] = done[i]

    def entering(f, rows):
        if f == GRAINS:
            return jnp.full((8, 128), melt_solute, f32)
        return jnp.where(marks[rows] == float(f), nucleus, 0.0)

    def received(tile, left, right, f, rows):
        tile = jnp.where(lane < 12, pltpu.roll(left, (-12 * f) % 128, 1), tile)
        tile = jnp.where((lane >= 108) & (lane < 120), pltpu.roll(right, (108 - 12 * f) % 128, 1), tile)
        edge = jnp.where(first_moves & enters, entering(f, rows), 0.0)
        return jnp.where(last, edge, tile)

    base = [received(packed[f, r], xl[r], xr[r], f, r) for f in range(FIELDS) for r in tiles]
    gather_own(F0, 2, E0m, base, 0, 20)
    halo = slice(16, 24)
    base = [received(eh[f], xlh[...], xrh[...], f, halo) for f in range(FIELDS)]
    gather_own(H0, 1, E0h, base, 1, 19)
    for f in range(FIELDS):
        E0h[f, 2:3] = E0m[f, 0:1]
        E0h[f, 4:5] = E0m[f, 15:16]

    rates = [step_rate * mob[g] for g in range(GRAINS)]
    keep = [1.0 - 6.0 * stiffness * r for r in rates]
    spreadrate = [stiffness * r for r in rates]

    def advance(c, beside, theta):
        squares = c[0] * c[0]
        for g in range(1, GRAINS):
            squares = squares + c[g] * c[g]
        s = c[GRAINS]
        well = squares - theta + coupling * s
        fresh = []
        after = None
        for g in range(GRAINS):
            new = c[g] * (keep[g] - rates[g] * well) + spreadrate[g] * beside[g]
            after = new * new if after is None else after + new * new
            fresh.append(new)
        solute = s * ((1.0 - 6.0 * diffusion) - rejection * (after - squares)) + diffusion * beside[GRAINS]
        return fresh + [solute]

    def theta_of(plane):
        return 1.0 - 2.0 * (plane.astype(f32) + 0.5) / (nz * 128.0)

    base_plane = gz * 128
    shift1 = jnp.full((8, 128), shifts[0], jnp.int32)
    theta_main = [theta_of(base_plane + lane - shift1), theta_of(base_plane + lane - 2)]
    theta_pack = [theta_of(base_plane + 126 + spot - shift1), theta_of(base_plane + 126 + spot - 2)]
    open_below = [~(lowest & first_moves & (lane == 2)), ~(lowest & (lane == 2))]
    final = lane == 127

    def rows_beside(above, tile, below, is_main):
        return jnp.where(row == 0, above, pltpu.roll(tile, 1, 0)) + jnp.where(row == 7, below, pltpu.roll(tile, 7, 0))

    def main_beside(F, H, E, f, xi, t, step):
        tile = F[f, xi, tiles[t]]
        other = F[f, xi, tiles[1 - t]]
        h = H[f, xi]
        if t == 0:
            above, below = pltpu.roll(h, 7, 0), pltpu.roll(other, 7, 0)
        else:
            above, below = pltpu.roll(other, 1, 0), pltpu.roll(h, 2, 0)
        beside = jnp.where(row == 0, above, pltpu.roll(tile, 1, 0)) + jnp.where(row == 7, below, pltpu.roll(tile, 7, 0))
        beside = beside + F[f, xi - 1, tiles[t]] + F[f, xi + 1, tiles[t]]
        nextplane = pltpu.roll(E[f, tiles[t]], 125 - 6 * xi, 1)
        beside = beside + jnp.where(open_below[step], pltpu.roll(tile, 1, 1), 0.0)
        return tile, beside + jnp.where(final, nextplane, pltpu.roll(tile, 127, 1))

    def halo_beside(f, xi):
        tile = H0[f, xi]
        beside = pltpu.roll(tile, 1, 0) + pltpu.roll(tile, 7, 0) + H0[f, xi - 1] + H0[f, xi + 1]
        nextplane = pltpu.roll(E0h[f], 125 - 6 * xi, 1)
        beside = beside + jnp.where(open_below[0], pltpu.roll(tile, 1, 1), 0.0)
        return tile, beside + jnp.where(final, nextplane, pltpu.roll(tile, 127, 1))

    def pack_beside(E, Eh, f, t):
        tile = E[f, tiles[t]]
        other = E[f, tiles[1 - t]]
        h = Eh[f]
        if t == 0:
            above, below = pltpu.roll(h, 7, 0), pltpu.roll(other, 7, 0)
        else:
            above, below = pltpu.roll(other, 1, 0), pltpu.roll(h, 2, 0)
        beside = jnp.where(row == 0, above, pltpu.roll(tile, 1, 0)) + jnp.where(row == 7, below, pltpu.roll(tile, 7, 0))
        return tile, beside + lanes_beside(tile)

    def lanes_beside(tile):
        return pltpu.roll(tile, 6, 1) + pltpu.roll(tile, 122, 1) + pltpu.roll(tile, 1, 1) + pltpu.roll(tile, 127, 1)

    def settle(new, f, rows):
        edge = jnp.where(enters, jnp.where(first_moves, new, entering(f, rows)), 0.0)
        return jnp.where(last & (spot >= 2), edge, new)

    def apply(pairs, theta):
        return advance([p[0] for p in pairs], [p[1] for p in pairs], theta)

    for t in range(2):
        new = apply([pack_beside(E0m, E0h, f, t) for f in range(FIELDS)], theta_pack[0])
        for f in range(FIELDS):
            E1m[f, tiles[t]] = settle(new[f], f, tiles[t])
    pairs = []
    for f in range(FIELDS):
        tile = E0h[f]
        pairs.append((tile, pltpu.roll(tile, 1, 0) + pltpu.roll(tile, 7, 0) + lanes_beside(tile)))
    new = apply(pairs, theta_pack[0])
    for f in range(FIELDS):
        E1h[f] = settle(new[f], f, halo)

    @pl.loop(1, 19)
    def _(xi):
        for t in range(2):
            new = apply([main_beside(F0, H0, E0m, f, xi, t, 0) for f in range(FIELDS)], theta_main[0])
            for f in range(FIELDS):
                F1[f, xi, tiles[t]] = new[f]

    @pl.loop(2, 18)
    def _(xi):
        new = apply([halo_beside(f, xi) for f in range(FIELDS)], theta_main[0])
        for f in range(FIELDS):
            H1[f, xi] = new[f]

    for t in range(2):
        new = apply([pack_beside(E1m, E1h, f, t) for f in range(FIELDS)], theta_pack[1])
        for f in range(FIELDS):
            E2m[f, tiles[t]] = new[f]

    @pl.loop(2, 18)
    def _(xi):
        for t in range(2):
            new = apply([main_beside(F1, H1, E1m, f, xi, t, 1) for f in range(FIELDS)], theta_main[1])
            for f in range(FIELDS):
                tail = pltpu.roll(E2m[f, tiles[t]], 124 - 6 * xi, 1)
                out[f, xi - 2, tiles[t]] = jnp.where(lane < 126, pltpu.roll(new[f], 126, 1), tail)


def shards(sizes, state, mobility, seeds, frame_shifts):
    V = pltpu.VMEM
    spec = pl.BlockSpec
    return pl.pallas_call(
        functools.partial(kernel, sizes),
        out_shape=jax.ShapeDtypeStruct(state.shape, f32),
        in_specs=[
            spec(memory_space=pltpu.SMEM),
            spec(memory_space=pltpu.SMEM),
            spec(memory_space=pl.ANY),
            spec(memory_space=pl.ANY),
        ],
        out_specs=spec(memory_space=pltpu.VMEM),
        scratch_shapes=[
            V((FIELDS, 20, 16, 128), f32),
            V((FIELDS, 20, 16, 128), f32),
            V((FIELDS, 20, 8, 128), f32),
            V((FIELDS, 20, 8, 128), f32),
            V((FIELDS, 8, 2, 128), f32),
            V((FIELDS + 2, 16, 128), f32),
            V((FIELDS + 2, 16, 128), f32),
            V((16, 128), f32),
            V((16, 128), f32),
            V((8, 128), f32),
            V((8, 128), f32),
            V((FIELDS, 8, 128), f32),
            V((FIELDS, 16, 128), f32),
            V((FIELDS, 8, 128), f32),
            V((FIELDS, 16, 128), f32),
            V((FIELDS, 8, 128), f32),
            V((FIELDS, 16, 128), f32),
            V((24, 128), f32),
            V(seeds.shape, jnp.int32),
            pltpu.SemaphoreType.DMA((4,)),
            pltpu.SemaphoreType.DMA((20,)),
            pltpu.SemaphoreType.DMA((20,)),
        ],
        compiler_params=pltpu.CompilerParams(collective_id=0, has_side_effects=True),
    )(mobility, frame_shifts, state, seeds)


def solution(mesh):
    sizes = tuple(mesh.shape[a] for a in ("gx", "gy", "gz"))
    placed = (P(None, "gx", "gy", "gz"), P(), P(), P())
    return jax.shard_map(
        functools.partial(shards, sizes), mesh=mesh, in_specs=placed, out_specs=P(None, "gx", "gy", "gz"), check_vma=False
    )
```

```python
import functools

import jax
import jax.numpy as jnp
from jax import lax
from jax.experimental import pallas as pl
from jax.experimental.pallas import tpu as pltpu
from jax.sharding import PartitionSpec as P

step_rate = 0.1
stiffness = 0.7
coupling = 0.5
diffusion = 0.14
rejection = 0.5
nucleus = 0.3
melt_solute = 1.0

MESH = pl.DeviceIdType.MESH
FIELDS = 9
GRAINS = 8
W = 16
COLUMN = 4
f32 = jnp.float32


def iota(shape, dim):
    return lax.broadcasted_iota(jnp.int32, shape, dim)


def kernel(sizes, mob, shifts, state, seeds, out, F0, F1, H0, H1, relay, pack, packed, xl, xr, xlh, xrh, eh,
           E0m, E0h, E1m, E1h, E2m, E2h, marks, seedbuf, local, send, recv):
    nx, ny, nz = sizes
    gx, gy, gz = lax.axis_index("gx"), lax.axis_index("gy"), lax.axis_index("gz")
    col = lax.rem(gy, COLUMN)

    def at(dx, dy, dz=0):
        return (lax.rem(gx + dx + nx, nx), lax.rem(gy + dy + ny, ny), lax.rem(gz + dz + nz, nz))

    far = at(0, jnp.where(col >= 2, 2, -2))
    around = [at(1, 0), at(-1, 0), at(0, 1), at(0, -1), at(1, 1), at(1, -1), at(-1, 1), at(-1, -1)]
    partners = around + [at(0, 0, 1), at(0, 0, -1), far]

    barrier = pltpu.get_barrier_semaphore()
    for partner in partners:
        pl.semaphore_signal(barrier, inc=1, device_id=partner, device_id_type=MESH)

    own = [
        pltpu.make_async_copy(state, F0.at[:, 2:18], local.at[0]),
        pltpu.make_async_copy(state.at[:, :, 0:2], H0.at[:, 2:18, 2:4], local.at[1]),
        pltpu.make_async_copy(state.at[:, :, 14:16], H0.at[:, 2:18, 4:6], local.at[2]),
        pltpu.make_async_copy(seeds, seedbuf, local.at[3]),
    ]
    for copy in own:
        copy.start()

    lane = iota((8, 128), 1)
    row = iota((8, 128), 0)
    group = lane // 6
    spot = lane - 6 * group
    tiles = (slice(0, 8), slice(8, 16))
    halo = slice(16, 24)

    pl.semaphore_wait(barrier, len(partners))

    def remote(src, dst, s, r, device):
        return pltpu.make_async_remote_copy(
            src_ref=src, dst_ref=dst, send_sem=send.at[s], recv_sem=recv.at[r], device_id=device, device_id_type=MESH
        )

    A, B = slice(0, 8), slice(8, 16)
    hA, hB = slice(2, 10), slice(10, 18)
    top, bottom = slice(14, 16), slice(0, 2)
    up_a = remote(state.at[:, A, top], H0.at[:, hA, 0:2], 0, 0, at(0, 1))
    up_b = remote(state.at[:, B, top], H0.at[:, hB, 0:2], 1, 1, at(0, 1))
    down_a = remote(state.at[:, A, bottom], H0.at[:, hA, 6:8], 2, 2, at(0, -1))
    down_b = remote(state.at[:, B, bottom], H0.at[:, hB, 6:8], 3, 3, at(0, -1))
    up_r = remote(state.at[:, B, top], relay, 1, 4, at(0, -1))
    down_r = remote(state.at[:, B, bottom], relay, 3, 4, at(0, 1))
    on_up = remote(relay, H0.at[:, hB, 0:2], 4, 1, far)
    on_down = remote(relay, H0.at[:, hB, 6:8], 4, 3, far)
    sides = [
        remote(state.at[:, 14:16], F0.at[:, 0:2], 5, 5, at(1, 0)),
        remote(state.at[:, 0:2], F0.at[:, 18:20], 6, 6, at(-1, 0)),
    ]
    corners = [
        remote(state.at[:, 15:16, 15:16], H0.at[:, 1:2, 1:2], 7, 7, at(1, 1)),
        remote(state.at[:, 15:16, 0:1], H0.at[:, 1:2, 6:7], 8, 8, at(1, -1)),
        remote(state.at[:, 0:1, 15:16], H0.at[:, 18:19, 1:2], 9, 9, at(-1, 1)),
        remote(state.at[:, 0:1, 0:1], H0.at[:, 18:19, 6:7], 10, 10, at(-1, -1)),
    ]
    planes = remote(pack, packed, 11, 11, at(0, 0, -1))
    early = gy < ny // 2
    up_far, down_far = col == COLUMN - 1, col == 0

    @pl.when(early)
    def _():
        for copy in sides:
            copy.start()

    @pl.when(up_far)
    def _():
        up_r.start()
        up_a.start()

    @pl.when(down_far)
    def _():
        down_r.start()
        down_a.start()

    @pl.when(~up_far)
    def _():
        up_a.start()
        up_b.start()

    @pl.when(~down_far)
    def _():
        down_a.start()
        down_b.start()

    for copy in corners:
        copy.start()

    own[0].wait()
    for f in range(FIELDS):
        for t in range(2):
            acc = jnp.zeros((8, 128), f32)
            for x in range(W):
                moved = pltpu.roll(F0[f, x + 2, tiles[t]], 6 * (x + 2) + 2, 1)
                acc = jnp.where((group == x + 2) & (spot >= 2), moved, acc)
            pack[f, tiles[t]] = acc
    for t in range(2):
        low = jnp.zeros((8, 128), f32)
        high = jnp.zeros((8, 128), f32)
        for f in range(FIELDS):
            acc = pack[f, tiles[t]]
            here = lane // 12 == f
            low = jnp.where(here, pltpu.roll(acc, (12 * f - 12) % 128, 1), low)
            high = jnp.where(here, pltpu.roll(acc, (12 * f - 96) % 128, 1), high)
        pack[FIELDS, tiles[t]] = low
        pack[FIELDS + 1, tiles[t]] = high

    own[3].wait()
    first_moves = jnp.full((8, 128), shifts[0], jnp.int32) == 2
    first_rows = jnp.full((256, 128), shifts[0], jnp.int32) == 2
    r24 = iota((24, 128), 0)
    offset = jnp.where(r24 < 16, r24, jnp.where(r24 < 20, r24 - 18, r24 - 6))
    wanted = lax.rem(gy * W + offset + ny * W, ny * W)
    pick = (iota((24, 128), 1) == wanted).astype(f32)
    xrow = iota((256, 128), 0)
    wlane = iota((256, 128), 1)
    wgroup = wlane // 6
    wspot = wlane - 6 * wgroup
    same = lax.rem(gx * W - 2 + wgroup + nx * W, nx * W) == xrow
    total = jnp.zeros((24, 128), f32)
    for k in range(2):
        grid = jnp.where(first_rows, seedbuf[0, k], seedbuf[1, k]).astype(f32)
        lines = lax.dot_general(pick, grid, (((1,), (1,)), ((), ())), preferred_element_type=f32)
        spread = (same & (wspot == 2 + k)).astype(f32)
        total = total + jnp.dot(lines, spread, preferred_element_type=f32)
    marks[...] = total

    planes.start()

    @pl.when(col == 2)
    def _():
        up_r.wait_recv()
        on_up.start()

    @pl.when(col == 1)
    def _():
        down_r.wait_recv()
        on_down.start()

    planes.wait_recv()
    second = [
        remote(packed.at[0:FIELDS, top], eh.at[:, 0:2], 12, 12, at(0, 1)),
        remote(packed.at[0:FIELDS, bottom], eh.at[:, 6:8], 13, 13, at(0, -1)),
        remote(packed.at[FIELDS + 1, 15:16], xlh.at[1:2], 16, 16, at(1, 1)),
        remote(packed.at[FIELDS + 1, 0:1], xlh.at[6:7], 17, 17, at(1, -1)),
        remote(packed.at[FIELDS, 15:16], xrh.at[1:2], 18, 18, at(-1, 1)),
        remote(packed.at[FIELDS, 0:1], xrh.at[6:7], 19, 19, at(-1, -1)),
    ]
    second_sides = [
        remote(packed.at[FIELDS + 1], xl, 14, 14, at(1, 0)),
        remote(packed.at[FIELDS], xr, 15, 15, at(-1, 0)),
    ]
    for copy in second + second_sides:
        copy.start()

    last = jnp.full((8, 128), gz, jnp.int32) == nz - 1
    lowest = jnp.full((8, 128), gz, jnp.int32) == 0
    enters = (spot == 2) | (spot == 3)
    final = lane == 127

    rates = [step_rate * mob[g] for g in range(GRAINS)]
    keep = [1.0 - 6.0 * stiffness * r for r in rates]
    spreadrate = [stiffness * r for r in rates]

    def advance(pairs, theta):
        c = [p[0] for p in pairs]
        beside = [p[1] for p in pairs]
        squares = c[0] * c[0]
        for g in range(1, GRAINS):
            squares = squares + c[g] * c[g]
        s = c[GRAINS]
        well = squares - theta + coupling * s
        fresh = []
        after = None
        for g in range(GRAINS):
            new = c[g] * (keep[g] - rates[g] * well) + spreadrate[g] * beside[g]
            after = new * new if after is None else after + new * new
            fresh.append(new)
        solute = s * ((1.0 - 6.0 * diffusion) - rejection * (after - squares)) + diffusion * beside[GRAINS]
        return fresh + [solute]

    def theta_of(plane):
        return 1.0 - 2.0 * (plane.astype(f32) + 0.5) / (nz * 128.0)

    base_plane = gz * 128
    shift1 = jnp.full((8, 128), shifts[0], jnp.int32)
    theta_main = [theta_of(base_plane + lane - shift1), theta_of(base_plane + lane - 2)]
    theta_pack = [theta_of(base_plane + 126 + spot - shift1), theta_of(base_plane + 126 + spot - 2)]
    open_below = [~(lowest & first_moves & (lane == 2)), ~(lowest & (lane == 2))]

    def entering(f, rows):
        if f == GRAINS:
            return jnp.full((8, 128), melt_solute, f32)
        return jnp.where(marks[rows] == float(f), nucleus, 0.0)

    def at_top(tile, f, rows):
        edge = jnp.where(first_moves & enters, entering(f, rows), 0.0)
        return jnp.where(last & (spot >= 2), edge, tile)

    def settle(new, f, rows):
        edge = jnp.where(enters, jnp.where(first_moves, new, entering(f, rows)), 0.0)
        return jnp.where(last & (spot >= 2), edge, new)

    def own_planes(acc, tile, xi):
        return jnp.where((group == xi) & (spot < 2), pltpu.roll(tile, (6 * xi + 2) % 128, 1), acc)

    def side_planes(tile, left, right, f):
        tile = jnp.where(lane < 12, pltpu.roll(left, (-12 * f) % 128, 1), tile)
        return jnp.where((lane >= 108) & (lane < 120), pltpu.roll(right, (108 - 12 * f) % 128, 1), tile)

    def rows_beside(F, index, t, f):
        tile = F[index + (tiles[t],)]
        other = F[index + (tiles[1 - t],)]
        if t == 0:
            return tile, pltpu.roll(tile, 1, 0) + jnp.where(row == 7, pltpu.roll(other, 7, 0), pltpu.roll(tile, 7, 0))
        return tile, jnp.where(row == 0, pltpu.roll(other, 1, 0), pltpu.roll(tile, 1, 0)) + pltpu.roll(tile, 7, 0)

    def planes_beside(tile, packed_tile, xi, step):
        nextplane = pltpu.roll(packed_tile, 125 - 6 * xi, 1)
        below = jnp.where(open_below[step], pltpu.roll(tile, 1, 1), 0.0)
        return below + jnp.where(final, nextplane, pltpu.roll(tile, 127, 1))

    def lanes_beside(tile):
        return pltpu.roll(tile, 6, 1) + pltpu.roll(tile, 122, 1) + pltpu.roll(tile, 1, 1) + pltpu.roll(tile, 127, 1)

    def main_pair(F, E, f, xi, t, step):
        tile, beside = rows_beside(F, (f, xi), t, f)
        beside = beside + F[f, xi - 1, tiles[t]] + F[f, xi + 1, tiles[t]]
        return tile, beside + planes_beside(tile, E[f, tiles[t]], xi, step)

    def pack_pair(E, f, t):
        tile, beside = rows_beside(E, (f,), t, f)
        return tile, beside + lanes_beside(tile)

    def edge_pair(H, E, f, xi, step):
        tile = H[f, xi]
        beside = pltpu.roll(tile, 1, 0) + pltpu.roll(tile, 7, 0) + H[f, xi - 1] + H[f, xi + 1]
        return tile, beside + planes_beside(tile, E[f], xi, step)

    def edge_pack_pair(E, f):
        tile = E[f]
        return tile, pltpu.roll(tile, 1, 0) + pltpu.roll(tile, 7, 0) + lanes_beside(tile)

    def pack_steps(which):
        for t in range(2):
            if which == 1:
                new = advance([pack_pair(E0m, f, t) for f in range(FIELDS)], theta_pack[0])
                for f in range(FIELDS):
                    E1m[f, tiles[t]] = settle(new[f], f, tiles[t])
            else:
                new = advance([pack_pair(E1m, f, t) for f in range(FIELDS)], theta_pack[1])
                for f in range(FIELDS):
                    E2m[f, tiles[t]] = new[f]

    def main_first(xi):
        for t in range(2):
            new = advance([main_pair(F0, E0m, f, xi, t, 0) for f in range(FIELDS)], theta_main[0])
            for f in range(FIELDS):
                F1[f, xi, tiles[t]] = new[f]

    def ended(new, packed_tile, xi):
        return pltpu.roll(jnp.where(lane < 2, pltpu.roll(packed_tile, (126 - 6 * xi) % 128, 1), new), 126, 1)

    def main_second(xi):
        for t in range(2):
            new = advance([main_pair(F1, E1m, f, xi, t, 1) for f in range(FIELDS)], theta_main[1])
            for f in range(FIELDS):
                out[f, xi - 2, tiles[t]] = ended(new[f], E2m[f, tiles[t]], xi)

    def each(lo, hi, unroll, step):
        def body(i, carry):
            step(i)
            return carry

        lax.fori_loop(lo, hi, body, 0, unroll=unroll)

    for f in range(FIELDS):
        for t in range(2):
            tile = at_top(packed[f, tiles[t]], f, tiles[t])
            for xi in range(2, 18):
                tile = own_planes(tile, F0[f, xi, tiles[t]], xi)
            E0m[f, tiles[t]] = tile
    pack_steps(1)
    pack_steps(2)
    each(3, 17, 2, main_first)
    each(4, 16, 2, main_second)

    @pl.when(~early)
    def _():
        @pl.when(up_far)
        def _():
            up_r.wait_send()
            up_a.wait_send()

        @pl.when(down_far)
        def _():
            down_r.wait_send()
            down_a.wait_send()

        @pl.when((col == 1) | (col == 2))
        def _():
            on_up.wait_send()

        for copy in sides:
            copy.start()

    for copy in own[1:3]:
        copy.wait()
    for copy in sides + second_sides:
        copy.wait_recv()
    trims = [
        pltpu.make_async_copy(F0.at[:, lo:lo + 2, y:y + 2], H0.at[:, lo:lo + 2, r:r + 2], local.at[i])
        for i, (lo, y, r) in enumerate([(0, 0, 2), (0, 14, 4), (18, 0, 2), (18, 14, 4)])
    ]
    for copy in trims:
        copy.start()
    for f in range(FIELDS):
        for t in range(2):
            tile = side_planes(E0m[f, tiles[t]], xl[tiles[t]], xr[tiles[t]], f)
            tile = at_top(tile, f, tiles[t])
            for xi in (0, 1, 18, 19):
                tile = own_planes(tile, F0[f, xi, tiles[t]], xi)
            E0m[f, tiles[t]] = tile
    pack_steps(1)
    pack_steps(2)
    for xi in (1, 2, 17, 18):
        main_first(xi)
    for xi in (2, 3, 16, 17):
        main_second(xi)
    for copy in trims:
        copy.wait()

    for copy in corners + second:
        copy.wait_recv()
    up_a.wait_recv()
    down_a.wait_recv()
    up_b.wait_recv()
    down_b.wait_recv()

    inner = (row >= 2) & (row < 6)
    for f in range(FIELDS):
        tile = side_planes(eh[f], xlh[...], xrh[...], f)
        tile = at_top(tile, f, halo)
        mid = jnp.where(row < 4, pltpu.roll(E0m[f, 0:8], 2, 0), pltpu.roll(E0m[f, 8:16], 6, 0))
        for xi in range(1, 19):
            tile = own_planes(tile, H0[f, xi], xi)
        E0h[f] = jnp.where(inner, mid, tile)

    def between(new, t0, t1):
        first = jnp.where(row < 2, pltpu.roll(new, 7, 0), pltpu.roll(t0, 1, 0))
        second = jnp.where(row < 6, pltpu.roll(t1, 7, 0), pltpu.roll(new, 1, 0))
        return jnp.where(row < 4, first, second)

    new = advance([edge_pack_pair(E0h, f) for f in range(FIELDS)], theta_pack[0])
    for f in range(FIELDS):
        E1h[f] = between(settle(new[f], f, halo), E1m[f, 0:8], E1m[f, 8:16])

    def edge_first(xi):
        new = advance([edge_pair(H0, E0h, f, xi, 0) for f in range(FIELDS)], theta_main[0])
        for f in range(FIELDS):
            H1[f, xi] = between(new[f], F1[f, xi, 0:8], F1[f, xi, 8:16])

    each(1, 19, 3, edge_first)
    new = advance([edge_pack_pair(E1h, f) for f in range(FIELDS)], theta_pack[1])
    for f in range(FIELDS):
        E2h[f] = new[f]

    def edge_second(xi):
        new = advance([edge_pair(H1, E1h, f, xi, 1) for f in range(FIELDS)], theta_main[1])
        for f in range(FIELDS):
            tile = ended(new[f], E2h[f], xi)
            out[f, xi - 2, 0:2] = tile[1:3]
            out[f, xi - 2, 14:16] = tile[5:7]

    each(2, 18, 4, edge_second)

    for copy in corners + second + second_sides + [planes]:
        copy.wait_send()

    @pl.when(early)
    def _():
        @pl.when((col == 1) | (col == 2))
        def _():
            on_up.wait_send()

        @pl.when(up_far)
        def _():
            up_r.wait_send()
            up_a.wait_send()

        @pl.when(down_far)
        def _():
            down_r.wait_send()
            down_a.wait_send()

    @pl.when(~up_far)
    def _():
        up_a.wait_send()
        up_b.wait_send()

    @pl.when(~down_far)
    def _():
        down_a.wait_send()
        down_b.wait_send()

    for copy in sides:
        copy.wait_send()


def shards(sizes, state, mobility, seeds, frame_shifts):
    V = pltpu.VMEM
    spec = pl.BlockSpec
    return pl.pallas_call(
        functools.partial(kernel, sizes),
        out_shape=jax.ShapeDtypeStruct(state.shape, f32),
        in_specs=[
            spec(memory_space=pltpu.SMEM),
            spec(memory_space=pltpu.SMEM),
            spec(memory_space=pl.ANY),
            spec(memory_space=pl.ANY),
        ],
        out_specs=spec(memory_space=pltpu.VMEM),
        scratch_shapes=[
            V((FIELDS, 20, 16, 128), f32),
            V((FIELDS, 20, 16, 128), f32),
            V((FIELDS, 20, 8, 128), f32),
            V((FIELDS, 20, 8, 128), f32),
            V((FIELDS, 8, 2, 128), f32),
            V((FIELDS + 2, 16, 128), f32),
            V((FIELDS + 2, 16, 128), f32),
            V((16, 128), f32),
            V((16, 128), f32),
            V((8, 128), f32),
            V((8, 128), f32),
            V((FIELDS, 8, 128), f32),
            V((FIELDS, 16, 128), f32),
            V((FIELDS, 8, 128), f32),
            V((FIELDS, 16, 128), f32),
            V((FIELDS, 8, 128), f32),
            V((FIELDS, 16, 128), f32),
            V((FIELDS, 8, 128), f32),
            V((24, 128), f32),
            V(seeds.shape, jnp.int32),
            pltpu.SemaphoreType.DMA((4,)),
            pltpu.SemaphoreType.DMA((20,)),
            pltpu.SemaphoreType.DMA((20,)),
        ],
        compiler_params=pltpu.CompilerParams(collective_id=0, has_side_effects=True),
    )(mobility, frame_shifts, state, seeds)


def solution(mesh):
    sizes = tuple(mesh.shape[a] for a in ("gx", "gy", "gz"))
    placed = (P(None, "gx", "gy", "gz"), P(), P(), P())
    return jax.shard_map(
        functools.partial(shards, sizes), mesh=mesh, in_specs=placed, out_specs=P(None, "gx", "gy", "gz"), check_vma=False
    )
```

```python
import functools

import jax
import jax.numpy as jnp
from jax import lax
from jax.experimental import pallas as pl
from jax.experimental.pallas import tpu as pltpu
from jax.sharding import PartitionSpec as P

step_rate = 0.1
stiffness = 0.7
coupling = 0.5
diffusion = 0.14
rejection = 0.5
nucleus = 0.3
melt_solute = 1.0

MESH = pl.DeviceIdType.MESH
FIELDS = 9
GRAINS = 8
W = 16
COLUMN = 4
f32 = jnp.float32


def iota(shape, dim):
    return lax.broadcasted_iota(jnp.int32, shape, dim)


def kernel(sizes, mob, shifts, state, seeds, out, F0, F1, H0, H1, relay, pack, packed, xl, xr, xlh, xrh, eh,
           E0m, E0h, E1m, E1h, E2m, E2h, marks, seedbuf, local, send, recv,
           far_ready, ring_ready):
    nx, ny, nz = sizes
    gx, gy, gz = lax.axis_index("gx"), lax.axis_index("gy"), lax.axis_index("gz")
    col = lax.rem(gy, COLUMN)

    def at(dx, dy, dz=0):
        return (lax.rem(gx + dx + nx, nx), lax.rem(gy + dy + ny, ny), lax.rem(gz + dz + nz, nz))

    early = gy < ny // 2
    far = at(0, jnp.where(col >= 2, 2, -2))
    around = [(1, 0), (-1, 0), (0, 1), (0, -1), (1, 1), (1, -1), (-1, 1), (-1, -1)]
    up_far, down_far = col == COLUMN - 1, col == 0
    middle = (col == 1) | (col == 2)

    def crosses(dy):
        return up_far if dy == 1 else down_far

    barrier = pltpu.get_barrier_semaphore()

    def tell(semaphore, device):
        pl.semaphore_signal(semaphore, inc=1, device_id=device, device_id_type=MESH)

    for dz in (1, -1):
        tell(barrier, at(0, 0, dz))
    for dx, dy in around:
        silent = (gx == nx - 1) if dx == 1 else None
        if dy:
            cross = crosses(dy)
            held = cross & ~early
            if silent is not None:
                held = held | (~cross & silent)
        else:
            held = silent
        if held is None:
            tell(barrier, at(dx, dy))
        else:
            @pl.when(~held)
            def _(dx=dx, dy=dy):
                tell(barrier, at(dx, dy))

    @pl.when(early)
    def _():
        tell(barrier, far)

    own = [
        pltpu.make_async_copy(state, F0.at[:, 2:18], local.at[0]),
        pltpu.make_async_copy(state.at[:, :, 0:2], H0.at[:, 2:18, 2:4], local.at[1]),
        pltpu.make_async_copy(state.at[:, :, 14:16], H0.at[:, 2:18, 4:6], local.at[2]),
        pltpu.make_async_copy(seeds, seedbuf, local.at[3]),
    ]
    for copy in own:
        copy.start()

    lane = iota((8, 128), 1)
    row = iota((8, 128), 0)
    group = lane // 6
    spot = lane - 6 * group
    tiles = (slice(0, 8), slice(8, 16))
    halo = slice(16, 24)

    n_far = jnp.where(middle, 1, 4)
    n_ring = jnp.where(middle, 3, 2)
    first_end, last_end = gx == 0, gx == nx - 1
    n_near = 11 - n_far - jnp.where(first_end | last_end, n_ring, 0)
    pl.semaphore_wait(barrier, n_near + jnp.where(early, 0, n_far) + jnp.where(last_end, n_ring, 0))

    @pl.when(~early)
    def _():
        tell(far_ready, far)
        for dy in (1, -1):
            @pl.when(crosses(dy))
            def _(dy=dy):
                for dx in (-1, 0, 1):
                    tell(far_ready, at(dx, dy))

    @pl.when(last_end)
    def _():
        tell(ring_ready, at(1, 0))
        for dy in (1, -1):
            @pl.when(~crosses(dy))
            def _(dy=dy):
                tell(ring_ready, at(1, dy))

    def remote(src, dst, s, r, device):
        return pltpu.make_async_remote_copy(
            src_ref=src, dst_ref=dst, send_sem=send.at[s], recv_sem=recv.at[r], device_id=device, device_id_type=MESH
        )

    A, B = slice(0, 8), slice(8, 16)
    hA, hB = slice(2, 10), slice(10, 18)
    top, bottom = slice(14, 16), slice(0, 2)
    up_a = remote(state.at[:, A, top], H0.at[:, hA, 0:2], 0, 0, at(0, 1))
    up_b = remote(state.at[:, B, top], H0.at[:, hB, 0:2], 1, 1, at(0, 1))
    down_a = remote(state.at[:, A, bottom], H0.at[:, hA, 6:8], 2, 2, at(0, -1))
    down_b = remote(state.at[:, B, bottom], H0.at[:, hB, 6:8], 3, 3, at(0, -1))
    up_r = remote(state.at[:, B, top], relay, 1, 4, at(0, -1))
    down_r = remote(state.at[:, B, bottom], relay, 3, 4, at(0, 1))
    on_up = remote(relay, H0.at[:, hB, 0:2], 4, 1, far)
    on_down = remote(relay, H0.at[:, hB, 6:8], 4, 3, far)
    sides = [
        remote(state.at[:, 14:16], F0.at[:, 0:2], 5, 5, at(1, 0)),
        remote(state.at[:, 0:2], F0.at[:, 18:20], 6, 6, at(-1, 0)),
    ]
    corners = [
        remote(state.at[:, 15:16, 15:16], H0.at[:, 1:2, 1:2], 7, 7, at(1, 1)),
        remote(state.at[:, 15:16, 0:1], H0.at[:, 1:2, 6:7], 8, 8, at(1, -1)),
        remote(state.at[:, 0:1, 15:16], H0.at[:, 18:19, 1:2], 9, 9, at(-1, 1)),
        remote(state.at[:, 0:1, 0:1], H0.at[:, 18:19, 6:7], 10, 10, at(-1, -1)),
    ]
    planes = remote(pack, packed, 11, 11, at(0, 0, -1))

    def begin(copies, when):
        for (dx, dy), copy in copies:
            cross = crosses(dy) if dy else jnp.bool_(False)
            waits_far = cross & early
            waits_ring = (first_end & ~cross) if dx == -1 else jnp.bool_(False)
            cond = [~waits_far & ~waits_ring, waits_ring, waits_far][when]

            @pl.when(cond)
            def _(copy=copy):
                copy.start()

    turns = [(1, 1), (1, -1), (-1, 1), (-1, -1)]
    corners_to = list(zip(turns, corners))
    sides_to = list(zip([(1, 0), (-1, 0)], sides))

    @pl.when(up_far)
    def _():
        up_r.start()

    @pl.when(down_far)
    def _():
        down_r.start()

    def send_far():
        @pl.when(up_far)
        def _():
            up_a.start()

        @pl.when(down_far)
        def _():
            down_a.start()

    @pl.when(~early)
    def _():
        send_far()

    @pl.when(early)
    def _():
        begin(sides_to, 0)

    @pl.when(~up_far)
    def _():
        up_a.start()
        up_b.start()

    @pl.when(~down_far)
    def _():
        down_a.start()
        down_b.start()

    begin(corners_to, 0)

    own[0].wait()
    for f in range(FIELDS):
        for t in range(2):
            acc = jnp.zeros((8, 128), f32)
            for x in range(W):
                moved = pltpu.roll(F0[f, x + 2, tiles[t]], 6 * (x + 2) + 2, 1)
                acc = jnp.where((group == x + 2) & (spot >= 2), moved, acc)
            pack[f, tiles[t]] = acc
    for t in range(2):
        low = jnp.zeros((8, 128), f32)
        high = jnp.zeros((8, 128), f32)
        for f in range(FIELDS):
            acc = pack[f, tiles[t]]
            here = lane // 12 == f
            low = jnp.where(here, pltpu.roll(acc, (12 * f - 12) % 128, 1), low)
            high = jnp.where(here, pltpu.roll(acc, (12 * f - 96) % 128, 1), high)
        pack[FIELDS, tiles[t]] = low
        pack[FIELDS + 1, tiles[t]] = high

    own[3].wait()
    first_moves = jnp.full((8, 128), shifts[0], jnp.int32) == 2
    first_rows = jnp.full((256, 128), shifts[0], jnp.int32) == 2
    r24 = iota((24, 128), 0)
    offset = jnp.where(r24 < 16, r24, jnp.where(r24 < 20, r24 - 18, r24 - 6))
    wanted = lax.rem(gy * W + offset + ny * W, ny * W)
    pick = (iota((24, 128), 1) == wanted).astype(f32)
    xrow = iota((256, 128), 0)
    wlane = iota((256, 128), 1)
    wgroup = wlane // 6
    wspot = wlane - 6 * wgroup
    same = lax.rem(gx * W - 2 + wgroup + nx * W, nx * W) == xrow
    total = jnp.zeros((24, 128), f32)
    for k in range(2):
        grid = jnp.where(first_rows, seedbuf[0, k], seedbuf[1, k]).astype(f32)
        lines = lax.dot_general(pick, grid, (((1,), (1,)), ((), ())), preferred_element_type=f32)
        spread = (same & (wspot == 2 + k)).astype(f32)
        total = total + jnp.dot(lines, spread, preferred_element_type=f32)
    marks[...] = total

    planes.start()

    def pass_on():
        @pl.when(col == 2)
        def _():
            up_r.wait_recv()
            on_up.start()

        @pl.when(col == 1)
        def _():
            down_r.wait_recv()
            on_down.start()

    @pl.when(~early)
    def _():
        pass_on()

    planes.wait_recv()
    second = [
        remote(packed.at[0:FIELDS, top], eh.at[:, 0:2], 12, 12, at(0, 1)),
        remote(packed.at[0:FIELDS, bottom], eh.at[:, 6:8], 13, 13, at(0, -1)),
        remote(packed.at[FIELDS + 1, 15:16], xlh.at[1:2], 16, 16, at(1, 1)),
        remote(packed.at[FIELDS + 1, 0:1], xlh.at[6:7], 17, 17, at(1, -1)),
        remote(packed.at[FIELDS, 15:16], xrh.at[1:2], 18, 18, at(-1, 1)),
        remote(packed.at[FIELDS, 0:1], xrh.at[6:7], 19, 19, at(-1, -1)),
    ]
    second_sides = [
        remote(packed.at[FIELDS + 1], xl, 14, 14, at(1, 0)),
        remote(packed.at[FIELDS], xr, 15, 15, at(-1, 0)),
    ]
    second_to = list(zip([(0, 1), (0, -1)] + turns, second)) + list(zip([(1, 0), (-1, 0)], second_sides))
    begin(second_to, 0)

    last = jnp.full((8, 128), gz, jnp.int32) == nz - 1
    lowest = jnp.full((8, 128), gz, jnp.int32) == 0
    enters = (spot == 2) | (spot == 3)
    final = lane == 127

    rates = [step_rate * mob[g] for g in range(GRAINS)]
    keep = [1.0 - 6.0 * stiffness * r for r in rates]
    spreadrate = [stiffness * r for r in rates]

    def advance(pairs, theta):
        c = [p[0] for p in pairs]
        beside = [p[1] for p in pairs]
        squares = c[0] * c[0]
        for g in range(1, GRAINS):
            squares = squares + c[g] * c[g]
        s = c[GRAINS]
        well = squares - theta + coupling * s
        fresh = []
        after = None
        for g in range(GRAINS):
            new = c[g] * (keep[g] - rates[g] * well) + spreadrate[g] * beside[g]
            after = new * new if after is None else after + new * new
            fresh.append(new)
        solute = s * ((1.0 - 6.0 * diffusion) - rejection * (after - squares)) + diffusion * beside[GRAINS]
        return fresh + [solute]

    def theta_of(plane):
        return 1.0 - 2.0 * (plane.astype(f32) + 0.5) / (nz * 128.0)

    base_plane = gz * 128
    shift1 = jnp.full((8, 128), shifts[0], jnp.int32)
    theta_main = [theta_of(base_plane + lane - shift1), theta_of(base_plane + lane - 2)]
    theta_pack = [theta_of(base_plane + 126 + spot - shift1), theta_of(base_plane + 126 + spot - 2)]
    open_below = [~(lowest & first_moves & (lane == 2)), ~(lowest & (lane == 2))]

    def entering(f, rows):
        if f == GRAINS:
            return jnp.full((8, 128), melt_solute, f32)
        return jnp.where(marks[rows] == float(f), nucleus, 0.0)

    def at_top(tile, f, rows):
        edge = jnp.where(first_moves & enters, entering(f, rows), 0.0)
        return jnp.where(last & (spot >= 2), edge, tile)

    def settle(new, f, rows):
        edge = jnp.where(enters, jnp.where(first_moves, new, entering(f, rows)), 0.0)
        return jnp.where(last & (spot >= 2), edge, new)

    def own_planes(acc, tile, xi):
        return jnp.where((group == xi) & (spot < 2), pltpu.roll(tile, (6 * xi + 2) % 128, 1), acc)

    def side_planes(tile, left, right, f):
        tile = jnp.where(lane < 12, pltpu.roll(left, (-12 * f) % 128, 1), tile)
        return jnp.where((lane >= 108) & (lane < 120), pltpu.roll(right, (108 - 12 * f) % 128, 1), tile)

    def rows_beside(F, index, t, f):
        tile = F[index + (tiles[t],)]
        other = F[index + (tiles[1 - t],)]
        if t == 0:
            return tile, pltpu.roll(tile, 1, 0) + jnp.where(row == 7, pltpu.roll(other, 7, 0), pltpu.roll(tile, 7, 0))
        return tile, jnp.where(row == 0, pltpu.roll(other, 1, 0), pltpu.roll(tile, 1, 0)) + pltpu.roll(tile, 7, 0)

    def planes_beside(tile, packed_tile, xi, step):
        nextplane = pltpu.roll(packed_tile, 125 - 6 * xi, 1)
        below = jnp.where(open_below[step], pltpu.roll(tile, 1, 1), 0.0)
        return below + jnp.where(final, nextplane, pltpu.roll(tile, 127, 1))

    def lanes_beside(tile):
        return pltpu.roll(tile, 6, 1) + pltpu.roll(tile, 122, 1) + pltpu.roll(tile, 1, 1) + pltpu.roll(tile, 127, 1)

    def main_pair(F, E, f, xi, t, step):
        tile, beside = rows_beside(F, (f, xi), t, f)
        beside = beside + F[f, xi - 1, tiles[t]] + F[f, xi + 1, tiles[t]]
        return tile, beside + planes_beside(tile, E[f, tiles[t]], xi, step)

    def pack_pair(E, f, t):
        tile, beside = rows_beside(E, (f,), t, f)
        return tile, beside + lanes_beside(tile)

    def edge_pair(H, E, f, xi, step):
        tile = H[f, xi]
        beside = pltpu.roll(tile, 1, 0) + pltpu.roll(tile, 7, 0) + H[f, xi - 1] + H[f, xi + 1]
        return tile, beside + planes_beside(tile, E[f], xi, step)

    def edge_pack_pair(E, f):
        tile = E[f]
        return tile, pltpu.roll(tile, 1, 0) + pltpu.roll(tile, 7, 0) + lanes_beside(tile)

    def pack_steps(which):
        for t in range(2):
            if which == 1:
                new = advance([pack_pair(E0m, f, t) for f in range(FIELDS)], theta_pack[0])
                for f in range(FIELDS):
                    E1m[f, tiles[t]] = settle(new[f], f, tiles[t])
            else:
                new = advance([pack_pair(E1m, f, t) for f in range(FIELDS)], theta_pack[1])
                for f in range(FIELDS):
                    E2m[f, tiles[t]] = new[f]

    def main_first(xi):
        for t in range(2):
            new = advance([main_pair(F0, E0m, f, xi, t, 0) for f in range(FIELDS)], theta_main[0])
            for f in range(FIELDS):
                F1[f, xi, tiles[t]] = new[f]

    def ended(new, packed_tile, xi):
        return pltpu.roll(jnp.where(lane < 2, pltpu.roll(packed_tile, (126 - 6 * xi) % 128, 1), new), 126, 1)

    def main_second(xi):
        for t in range(2):
            new = advance([main_pair(F1, E1m, f, xi, t, 1) for f in range(FIELDS)], theta_main[1])
            for f in range(FIELDS):
                out[f, xi - 2, tiles[t]] = ended(new[f], E2m[f, tiles[t]], xi)

    def each(lo, hi, unroll, step):
        def body(i, carry):
            step(i)
            return carry

        lax.fori_loop(lo, hi, body, 0, unroll=unroll)

    for f in range(FIELDS):
        for t in range(2):
            tile = at_top(packed[f, tiles[t]], f, tiles[t])
            for xi in range(2, 18):
                tile = own_planes(tile, F0[f, xi, tiles[t]], xi)
            E0m[f, tiles[t]] = tile
    pack_steps(1)
    pack_steps(2)
    each(3, 17, 2, main_first)
    each(4, 16, 2, main_second)

    @pl.when(~early)
    def _():
        @pl.when(up_far)
        def _():
            up_r.wait_send()
            up_a.wait_send()

        @pl.when(down_far)
        def _():
            down_r.wait_send()
            down_a.wait_send()

        @pl.when(middle)
        def _():
            on_up.wait_send()

        begin(sides_to, 0)

    @pl.when(first_end)
    def _():
        pl.semaphore_wait(ring_ready, n_ring)
        begin(sides_to, 1)
        begin(corners_to, 1)
        begin(second_to, 1)

    @pl.when(early)
    def _():
        pl.semaphore_wait(far_ready, n_far)
        send_far()
        begin(corners_to, 2)
        begin(second_to, 2)
        pass_on()

    for copy in own[1:3]:
        copy.wait()
    for copy in sides + second_sides:
        copy.wait_recv()
    trims = [
        pltpu.make_async_copy(F0.at[:, lo:lo + 2, y:y + 2], H0.at[:, lo:lo + 2, r:r + 2], local.at[i])
        for i, (lo, y, r) in enumerate([(0, 0, 2), (0, 14, 4), (18, 0, 2), (18, 14, 4)])
    ]
    for copy in trims:
        copy.start()
    for f in range(FIELDS):
        for t in range(2):
            tile = side_planes(E0m[f, tiles[t]], xl[tiles[t]], xr[tiles[t]], f)
            tile = at_top(tile, f, tiles[t])
            for xi in (0, 1, 18, 19):
                tile = own_planes(tile, F0[f, xi, tiles[t]], xi)
            E0m[f, tiles[t]] = tile
    pack_steps(1)
    pack_steps(2)
    for xi in (1, 2, 17, 18):
        main_first(xi)
    for xi in (2, 3, 16, 17):
        main_second(xi)
    for copy in trims:
        copy.wait()

    for copy in corners + second:
        copy.wait_recv()
    up_a.wait_recv()
    down_a.wait_recv()
    up_b.wait_recv()
    down_b.wait_recv()

    inner = (row >= 2) & (row < 6)
    for f in range(FIELDS):
        tile = side_planes(eh[f], xlh[...], xrh[...], f)
        tile = at_top(tile, f, halo)
        mid = jnp.where(row < 4, pltpu.roll(E0m[f, 0:8], 2, 0), pltpu.roll(E0m[f, 8:16], 6, 0))
        for xi in range(1, 19):
            tile = own_planes(tile, H0[f, xi], xi)
        E0h[f] = jnp.where(inner, mid, tile)

    def between(new, t0, t1):
        first = jnp.where(row < 2, pltpu.roll(new, 7, 0), pltpu.roll(t0, 1, 0))
        second = jnp.where(row < 6, pltpu.roll(t1, 7, 0), pltpu.roll(new, 1, 0))
        return jnp.where(row < 4, first, second)

    new = advance([edge_pack_pair(E0h, f) for f in range(FIELDS)], theta_pack[0])
    for f in range(FIELDS):
        E1h[f] = between(settle(new[f], f, halo), E1m[f, 0:8], E1m[f, 8:16])

    def edge_first(xi):
        new = advance([edge_pair(H0, E0h, f, xi, 0) for f in range(FIELDS)], theta_main[0])
        for f in range(FIELDS):
            H1[f, xi] = between(new[f], F1[f, xi, 0:8], F1[f, xi, 8:16])

    each(1, 19, 3, edge_first)
    new = advance([edge_pack_pair(E1h, f) for f in range(FIELDS)], theta_pack[1])
    for f in range(FIELDS):
        E2h[f] = new[f]

    def edge_second(xi):
        new = advance([edge_pair(H1, E1h, f, xi, 1) for f in range(FIELDS)], theta_main[1])
        for f in range(FIELDS):
            tile = ended(new[f], E2h[f], xi)
            out[f, xi - 2, 0:2] = tile[1:3]
            out[f, xi - 2, 14:16] = tile[5:7]

    each(2, 18, 4, edge_second)

    for copy in corners + second + second_sides + [planes]:
        copy.wait_send()

    @pl.when(early)
    def _():
        @pl.when(middle)
        def _():
            on_up.wait_send()

        @pl.when(up_far)
        def _():
            up_r.wait_send()
            up_a.wait_send()

        @pl.when(down_far)
        def _():
            down_r.wait_send()
            down_a.wait_send()

    @pl.when(~up_far)
    def _():
        up_a.wait_send()
        up_b.wait_send()

    @pl.when(~down_far)
    def _():
        down_a.wait_send()
        down_b.wait_send()

    for copy in sides:
        copy.wait_send()


def shards(sizes, state, mobility, seeds, frame_shifts):
    V = pltpu.VMEM
    spec = pl.BlockSpec
    return pl.pallas_call(
        functools.partial(kernel, sizes),
        out_shape=jax.ShapeDtypeStruct(state.shape, f32),
        in_specs=[
            spec(memory_space=pltpu.SMEM),
            spec(memory_space=pltpu.SMEM),
            spec(memory_space=pl.ANY),
            spec(memory_space=pl.ANY),
        ],
        out_specs=spec(memory_space=pltpu.VMEM),
        scratch_shapes=[
            V((FIELDS, 20, 16, 128), f32),
            V((FIELDS, 20, 16, 128), f32),
            V((FIELDS, 20, 8, 128), f32),
            V((FIELDS, 20, 8, 128), f32),
            V((FIELDS, 8, 2, 128), f32),
            V((FIELDS + 2, 16, 128), f32),
            V((FIELDS + 2, 16, 128), f32),
            V((16, 128), f32),
            V((16, 128), f32),
            V((8, 128), f32),
            V((8, 128), f32),
            V((FIELDS, 8, 128), f32),
            V((FIELDS, 16, 128), f32),
            V((FIELDS, 8, 128), f32),
            V((FIELDS, 16, 128), f32),
            V((FIELDS, 8, 128), f32),
            V((FIELDS, 16, 128), f32),
            V((FIELDS, 8, 128), f32),
            V((24, 128), f32),
            V(seeds.shape, jnp.int32),
            pltpu.SemaphoreType.DMA((4,)),
            pltpu.SemaphoreType.DMA((20,)),
            pltpu.SemaphoreType.DMA((20,)),
            pltpu.SemaphoreType.REGULAR,
            pltpu.SemaphoreType.REGULAR,
        ],
        compiler_params=pltpu.CompilerParams(collective_id=0, has_side_effects=True),
    )(mobility, frame_shifts, state, seeds)


def solution(mesh):
    sizes = tuple(mesh.shape[a] for a in ("gx", "gy", "gz"))
    placed = (P(None, "gx", "gy", "gz"), P(), P(), P())
    return jax.shard_map(
        functools.partial(shards, sizes), mesh=mesh, in_specs=placed, out_specs=P(None, "gx", "gy", "gz"), check_vma=False
    )
```

```python
import functools

import jax
import jax.numpy as jnp
from jax import lax
from jax.experimental import pallas as pl
from jax.experimental.pallas import tpu as pltpu
from jax.sharding import PartitionSpec as P

step_rate = 0.1
stiffness = 0.7
coupling = 0.5
diffusion = 0.14
rejection = 0.5
nucleus = 0.3
melt_solute = 1.0

MESH = pl.DeviceIdType.MESH
FIELDS = 9
GRAINS = 8
W = 16
COLUMN = 4
f32 = jnp.float32


def iota(shape, dim):
    return lax.broadcasted_iota(jnp.int32, shape, dim)


def kernel(sizes, mob, shifts, state, seeds, out, F0, F1, H0, H1, relay, pack, packed, xl, xr, xlh, xrh, eh,
           E0m, E0h, E1m, E1h, E2m, E2h, marks, seedbuf, local, send, recv,
           far_ready, ring_ready):
    nx, ny, nz = sizes
    gx, gy, gz = lax.axis_index("gx"), lax.axis_index("gy"), lax.axis_index("gz")
    col = lax.rem(gy, COLUMN)

    def at(dx, dy, dz=0):
        return (lax.rem(gx + dx + nx, nx), lax.rem(gy + dy + ny, ny), lax.rem(gz + dz + nz, nz))

    early = gy < ny // 2
    far = at(0, jnp.where(col >= 2, 2, -2))
    around = [(1, 0), (-1, 0), (0, 1), (0, -1), (1, 1), (1, -1), (-1, 1), (-1, -1)]
    up_far, down_far = col == COLUMN - 1, col == 0
    middle = (col == 1) | (col == 2)

    def crosses(dy):
        return up_far if dy == 1 else down_far

    barrier = pltpu.get_barrier_semaphore()

    def tell(semaphore, device):
        pl.semaphore_signal(semaphore, inc=1, device_id=device, device_id_type=MESH)

    for dz in (1, -1):
        tell(barrier, at(0, 0, dz))
    for dx, dy in around:
        silent = (gx == nx - 1) if dx == 1 else None
        if dy:
            cross = crosses(dy)
            held = cross & ~early
            if silent is not None:
                held = held | (~cross & silent)
        else:
            held = silent
        if held is None:
            tell(barrier, at(dx, dy))
        else:
            @pl.when(~held)
            def _(dx=dx, dy=dy):
                tell(barrier, at(dx, dy))

    @pl.when(early)
    def _():
        tell(barrier, far)

    own = [
        pltpu.make_async_copy(state, F0.at[:, 2:18], local.at[0]),
        pltpu.make_async_copy(state.at[:, :, 0:2], H0.at[:, 2:18, 2:4], local.at[1]),
        pltpu.make_async_copy(state.at[:, :, 14:16], H0.at[:, 2:18, 4:6], local.at[2]),
        pltpu.make_async_copy(seeds, seedbuf, local.at[3]),
    ]
    for copy in own:
        copy.start()

    lane = iota((8, 128), 1)
    row = iota((8, 128), 0)
    group = lane // 6
    spot = lane - 6 * group
    tiles = (slice(0, 8), slice(8, 16))
    halo = slice(16, 24)

    n_far = jnp.where(middle, 1, 4)
    n_ring = jnp.where(middle, 3, 2)
    first_end, last_end = gx == 0, gx == nx - 1
    n_near = 11 - n_far - jnp.where(first_end | last_end, n_ring, 0)
    pl.semaphore_wait(barrier, n_near + jnp.where(early, 0, n_far) + jnp.where(last_end, n_ring, 0))

    @pl.when(~early)
    def _():
        tell(far_ready, far)
        for dy in (1, -1):
            @pl.when(crosses(dy))
            def _(dy=dy):
                for dx in (-1, 0, 1):
                    tell(far_ready, at(dx, dy))

    @pl.when(last_end)
    def _():
        tell(ring_ready, at(1, 0))
        for dy in (1, -1):
            @pl.when(~crosses(dy))
            def _(dy=dy):
                tell(ring_ready, at(1, dy))

    def remote(src, dst, s, r, device):
        return pltpu.make_async_remote_copy(
            src_ref=src, dst_ref=dst, send_sem=send.at[s], recv_sem=recv.at[r], device_id=device, device_id_type=MESH
        )

    A, B = slice(0, 8), slice(8, 16)
    hA, hB = slice(2, 10), slice(10, 18)
    top, bottom = slice(14, 16), slice(0, 2)
    up_a = remote(state.at[:, A, top], H0.at[:, hA, 0:2], 0, 0, at(0, 1))
    up_b = remote(state.at[:, B, top], H0.at[:, hB, 0:2], 1, 1, at(0, 1))
    down_a = remote(state.at[:, A, bottom], H0.at[:, hA, 6:8], 2, 2, at(0, -1))
    down_b = remote(state.at[:, B, bottom], H0.at[:, hB, 6:8], 3, 3, at(0, -1))
    up_r = remote(state.at[:, B, top], relay, 1, 4, at(0, -1))
    down_r = remote(state.at[:, B, bottom], relay, 3, 4, at(0, 1))
    on_up = remote(relay, H0.at[:, hB, 0:2], 4, 1, far)
    on_down = remote(relay, H0.at[:, hB, 6:8], 4, 3, far)
    sides = [
        remote(state.at[:, 14:16], F0.at[:, 0:2], 5, 5, at(1, 0)),
        remote(state.at[:, 0:2], F0.at[:, 18:20], 6, 6, at(-1, 0)),
    ]
    corners = [
        remote(state.at[:, 15:16, 15:16], H0.at[:, 1:2, 1:2], 7, 7, at(1, 1)),
        remote(state.at[:, 15:16, 0:1], H0.at[:, 1:2, 6:7], 8, 8, at(1, -1)),
        remote(state.at[:, 0:1, 15:16], H0.at[:, 18:19, 1:2], 9, 9, at(-1, 1)),
        remote(state.at[:, 0:1, 0:1], H0.at[:, 18:19, 6:7], 10, 10, at(-1, -1)),
    ]
    planes = remote(pack, packed, 11, 11, at(0, 0, -1))

    def begin(copies, when):
        for (dx, dy), copy in copies:
            cross = crosses(dy) if dy else jnp.bool_(False)
            waits_far = cross & early
            waits_ring = (first_end & ~cross) if dx == -1 else jnp.bool_(False)
            cond = [~waits_far & ~waits_ring, waits_ring, waits_far][when]

            @pl.when(cond)
            def _(copy=copy):
                copy.start()

    turns = [(1, 1), (1, -1), (-1, 1), (-1, -1)]
    corners_to = list(zip(turns, corners))
    sides_to = list(zip([(1, 0), (-1, 0)], sides))

    @pl.when(up_far)
    def _():
        up_r.start()

    @pl.when(down_far)
    def _():
        down_r.start()

    def send_far():
        @pl.when(up_far)
        def _():
            up_a.start()

        @pl.when(down_far)
        def _():
            down_a.start()

    @pl.when(~early)
    def _():
        send_far()

    @pl.when(early)
    def _():
        begin(sides_to, 0)

    @pl.when(~up_far)
    def _():
        up_a.start()
        up_b.start()

    @pl.when(~down_far)
    def _():
        down_a.start()
        down_b.start()

    begin(corners_to, 0)

    own[0].wait()
    for f in range(FIELDS):
        for t in range(2):
            acc = jnp.zeros((8, 128), f32)
            for x in range(W):
                moved = pltpu.roll(F0[f, x + 2, tiles[t]], 6 * (x + 2) + 2, 1)
                acc = jnp.where((group == x + 2) & (spot >= 2), moved, acc)
            pack[f, tiles[t]] = acc
    for t in range(2):
        low = jnp.zeros((8, 128), f32)
        high = jnp.zeros((8, 128), f32)
        for f in range(FIELDS):
            acc = pack[f, tiles[t]]
            here = lane // 12 == f
            low = jnp.where(here, pltpu.roll(acc, (12 * f - 12) % 128, 1), low)
            high = jnp.where(here, pltpu.roll(acc, (12 * f - 96) % 128, 1), high)
        pack[FIELDS, tiles[t]] = low
        pack[FIELDS + 1, tiles[t]] = high

    own[3].wait()
    first_moves = jnp.full((8, 128), shifts[0], jnp.int32) == 2
    first_rows = jnp.full((256, 128), shifts[0], jnp.int32) == 2
    r24 = iota((24, 128), 0)
    offset = jnp.where(r24 < 16, r24, jnp.where(r24 < 20, r24 - 18, r24 - 6))
    wanted = lax.rem(gy * W + offset + ny * W, ny * W)
    pick = (iota((24, 128), 1) == wanted).astype(f32)
    xrow = iota((256, 128), 0)
    wlane = iota((256, 128), 1)
    wgroup = wlane // 6
    wspot = wlane - 6 * wgroup
    same = lax.rem(gx * W - 2 + wgroup + nx * W, nx * W) == xrow
    total = jnp.zeros((24, 128), f32)
    for k in range(2):
        grid = jnp.where(first_rows, seedbuf[0, k], seedbuf[1, k]).astype(f32)
        lines = lax.dot_general(pick, grid, (((1,), (1,)), ((), ())), preferred_element_type=f32)
        spread = (same & (wspot == 2 + k)).astype(f32)
        total = total + jnp.dot(lines, spread, preferred_element_type=f32)
    marks[...] = total

    planes.start()

    def pass_on():
        @pl.when(col == 2)
        def _():
            up_r.wait_recv()
            on_up.start()

        @pl.when(col == 1)
        def _():
            down_r.wait_recv()
            on_down.start()

    @pl.when(~early)
    def _():
        pass_on()

    planes.wait_recv()
    second = [
        remote(packed.at[0:FIELDS, top], eh.at[:, 0:2], 12, 12, at(0, 1)),
        remote(packed.at[0:FIELDS, bottom], eh.at[:, 6:8], 13, 13, at(0, -1)),
        remote(packed.at[FIELDS + 1, 15:16], xlh.at[1:2], 16, 16, at(1, 1)),
        remote(packed.at[FIELDS + 1, 0:1], xlh.at[6:7], 17, 17, at(1, -1)),
        remote(packed.at[FIELDS, 15:16], xrh.at[1:2], 18, 18, at(-1, 1)),
        remote(packed.at[FIELDS, 0:1], xrh.at[6:7], 19, 19, at(-1, -1)),
    ]
    second_sides = [
        remote(packed.at[FIELDS + 1], xl, 14, 14, at(1, 0)),
        remote(packed.at[FIELDS], xr, 15, 15, at(-1, 0)),
    ]
    second_to = list(zip([(0, 1), (0, -1)] + turns, second)) + list(zip([(1, 0), (-1, 0)], second_sides))
    begin(second_to, 0)

    last = jnp.full((8, 128), gz, jnp.int32) == nz - 1
    lowest = jnp.full((8, 128), gz, jnp.int32) == 0
    enters = (spot == 2) | (spot == 3)
    final = lane == 127

    rates = [step_rate * mob[g] for g in range(GRAINS)]
    keep = [1.0 - 6.0 * stiffness * r for r in rates]
    spreadrate = [stiffness * r for r in rates]

    def advance(pairs, theta):
        c = [p[0] for p in pairs]
        beside = [p[1] for p in pairs]
        squares = c[0] * c[0]
        for g in range(1, GRAINS):
            squares = squares + c[g] * c[g]
        s = c[GRAINS]
        well = squares - theta + coupling * s
        fresh = []
        after = None
        for g in range(GRAINS):
            new = c[g] * (keep[g] - rates[g] * well) + spreadrate[g] * beside[g]
            after = new * new if after is None else after + new * new
            fresh.append(new)
        solute = s * ((1.0 - 6.0 * diffusion) - rejection * (after - squares)) + diffusion * beside[GRAINS]
        return fresh + [solute]

    def theta_of(plane):
        return 1.0 - 2.0 * (plane.astype(f32) + 0.5) / (nz * 128.0)

    base_plane = gz * 128
    shift1 = jnp.full((8, 128), shifts[0], jnp.int32)
    theta_main = [theta_of(base_plane + lane - shift1), theta_of(base_plane + lane - 2)]
    theta_pack = [theta_of(base_plane + 126 + spot - shift1), theta_of(base_plane + 126 + spot - 2)]
    open_below = [~(lowest & first_moves & (lane == 2)), ~(lowest & (lane == 2))]

    def entering(f, rows):
        if f == GRAINS:
            return jnp.full((8, 128), melt_solute, f32)
        return jnp.where(marks[rows] == float(f), nucleus, 0.0)

    def at_top(tile, f, rows):
        edge = jnp.where(first_moves & enters, entering(f, rows), 0.0)
        return jnp.where(last & (spot >= 2), edge, tile)

    def settle(new, f, rows):
        edge = jnp.where(enters, jnp.where(first_moves, new, entering(f, rows)), 0.0)
        return jnp.where(last & (spot >= 2), edge, new)

    def own_planes(acc, tile, xi):
        return jnp.where((group == xi) & (spot < 2), pltpu.roll(tile, (6 * xi + 2) % 128, 1), acc)

    def side_planes(tile, left, right, f):
        tile = jnp.where(lane < 12, pltpu.roll(left, (-12 * f) % 128, 1), tile)
        return jnp.where((lane >= 108) & (lane < 120), pltpu.roll(right, (108 - 12 * f) % 128, 1), tile)

    def rows_beside(F, index, t, f):
        tile = F[index + (tiles[t],)]
        other = F[index + (tiles[1 - t],)]
        if t == 0:
            return tile, pltpu.roll(tile, 1, 0) + jnp.where(row == 7, pltpu.roll(other, 7, 0), pltpu.roll(tile, 7, 0))
        return tile, jnp.where(row == 0, pltpu.roll(other, 1, 0), pltpu.roll(tile, 1, 0)) + pltpu.roll(tile, 7, 0)

    def planes_beside(tile, nextplane, step):
        below = jnp.where(open_below[step], pltpu.roll(tile, 1, 1), 0.0)
        return below + jnp.where(final, nextplane, pltpu.roll(tile, 127, 1))

    def lanes_beside(tile):
        return pltpu.roll(tile, 6, 1) + pltpu.roll(tile, 122, 1) + pltpu.roll(tile, 1, 1) + pltpu.roll(tile, 127, 1)

    def main_pair(F, ahead, f, xi, t, step):
        tile, beside = rows_beside(F, (f, xi), t, f)
        beside = beside + F[f, xi - 1, tiles[t]] + F[f, xi + 1, tiles[t]]
        return tile, beside + planes_beside(tile, ahead[f], step)

    def pack_pair(E, f, t):
        tile, beside = rows_beside(E, (f,), t, f)
        return tile, beside + lanes_beside(tile)

    def edge_pair(H, ahead, f, xi, step):
        tile = H[f, xi]
        beside = pltpu.roll(tile, 1, 0) + pltpu.roll(tile, 7, 0) + H[f, xi - 1] + H[f, xi + 1]
        return tile, beside + planes_beside(tile, ahead[f], step)

    def edge_pack_pair(E, f):
        tile = E[f]
        return tile, pltpu.roll(tile, 1, 0) + pltpu.roll(tile, 7, 0) + lanes_beside(tile)

    def pack_steps(which):
        for t in range(2):
            if which == 1:
                new = advance([pack_pair(E0m, f, t) for f in range(FIELDS)], theta_pack[0])
                for f in range(FIELDS):
                    E1m[f, tiles[t]] = settle(new[f], f, tiles[t])
            else:
                new = advance([pack_pair(E1m, f, t) for f in range(FIELDS)], theta_pack[1])
                for f in range(FIELDS):
                    E2m[f, tiles[t]] = joined(E1m[f, tiles[t]], new[f])

    def main_first(xi):
        for t in range(2):
            ahead = [pltpu.roll(E0m[f, tiles[t]], 125 - 6 * xi, 1) for f in range(FIELDS)]
            new = advance([main_pair(F0, ahead, f, xi, t, 0) for f in range(FIELDS)], theta_main[0])
            for f in range(FIELDS):
                F1[f, xi, tiles[t]] = new[f]

    def joined(first, second):
        return jnp.where(spot == 1, pltpu.roll(first, 127, 1), second)

    def ended(new, ahead):
        return pltpu.roll(jnp.where(lane < 2, ahead, new), 126, 1)

    def main_second(xi):
        for t in range(2):
            ahead = [pltpu.roll(E2m[f, tiles[t]], 126 - 6 * xi, 1) for f in range(FIELDS)]
            new = advance([main_pair(F1, ahead, f, xi, t, 1) for f in range(FIELDS)], theta_main[1])
            for f in range(FIELDS):
                out[f, xi - 2, tiles[t]] = ended(new[f], ahead[f])

    def each(lo, hi, unroll, step):
        def body(i, carry):
            step(i)
            return carry

        lax.fori_loop(lo, hi, body, 0, unroll=unroll)

    for f in range(FIELDS):
        for t in range(2):
            tile = at_top(packed[f, tiles[t]], f, tiles[t])
            for xi in range(2, 18):
                tile = own_planes(tile, F0[f, xi, tiles[t]], xi)
            E0m[f, tiles[t]] = tile
    pack_steps(1)
    pack_steps(2)
    each(3, 17, 2, main_first)
    each(4, 16, 2, main_second)

    @pl.when(~early)
    def _():
        @pl.when(up_far)
        def _():
            up_r.wait_send()
            up_a.wait_send()

        @pl.when(down_far)
        def _():
            down_r.wait_send()
            down_a.wait_send()

        @pl.when(middle)
        def _():
            on_up.wait_send()

        begin(sides_to, 0)

    @pl.when(first_end)
    def _():
        pl.semaphore_wait(ring_ready, n_ring)
        begin(sides_to, 1)
        begin(corners_to, 1)
        begin(second_to, 1)

    @pl.when(early)
    def _():
        pl.semaphore_wait(far_ready, n_far)
        send_far()
        begin(corners_to, 2)
        begin(second_to, 2)
        pass_on()

    for copy in own[1:3]:
        copy.wait()
    for copy in sides + second_sides:
        copy.wait_recv()
    trims = [
        pltpu.make_async_copy(F0.at[:, lo:lo + 2, y:y + 2], H0.at[:, lo:lo + 2, r:r + 2], local.at[i])
        for i, (lo, y, r) in enumerate([(0, 0, 2), (0, 14, 4), (18, 0, 2), (18, 14, 4)])
    ]
    for copy in trims:
        copy.start()
    for f in range(FIELDS):
        for t in range(2):
            tile = side_planes(E0m[f, tiles[t]], xl[tiles[t]], xr[tiles[t]], f)
            tile = at_top(tile, f, tiles[t])
            for xi in (0, 1, 18, 19):
                tile = own_planes(tile, F0[f, xi, tiles[t]], xi)
            E0m[f, tiles[t]] = tile
    pack_steps(1)
    pack_steps(2)
    for xi in (1, 2, 17, 18):
        main_first(xi)
    for xi in (2, 3, 16, 17):
        main_second(xi)
    for copy in trims:
        copy.wait()

    for copy in corners + second:
        copy.wait_recv()
    up_a.wait_recv()
    down_a.wait_recv()
    up_b.wait_recv()
    down_b.wait_recv()

    inner = (row >= 2) & (row < 6)
    for f in range(FIELDS):
        tile = side_planes(eh[f], xlh[...], xrh[...], f)
        tile = at_top(tile, f, halo)
        mid = jnp.where(row < 4, pltpu.roll(E0m[f, 0:8], 2, 0), pltpu.roll(E0m[f, 8:16], 6, 0))
        for xi in range(1, 19):
            tile = own_planes(tile, H0[f, xi], xi)
        E0h[f] = jnp.where(inner, mid, tile)

    def between(new, t0, t1):
        first = jnp.where(row < 2, pltpu.roll(new, 7, 0), pltpu.roll(t0, 1, 0))
        second = jnp.where(row < 6, pltpu.roll(t1, 7, 0), pltpu.roll(new, 1, 0))
        return jnp.where(row < 4, first, second)

    new = advance([edge_pack_pair(E0h, f) for f in range(FIELDS)], theta_pack[0])
    for f in range(FIELDS):
        E1h[f] = between(settle(new[f], f, halo), E1m[f, 0:8], E1m[f, 8:16])

    def edge_first(xi):
        ahead = [pltpu.roll(E0h[f], 125 - 6 * xi, 1) for f in range(FIELDS)]
        new = advance([edge_pair(H0, ahead, f, xi, 0) for f in range(FIELDS)], theta_main[0])
        for f in range(FIELDS):
            H1[f, xi] = between(new[f], F1[f, xi, 0:8], F1[f, xi, 8:16])

    each(1, 19, 3, edge_first)
    new = advance([edge_pack_pair(E1h, f) for f in range(FIELDS)], theta_pack[1])
    for f in range(FIELDS):
        E2h[f] = joined(E1h[f], new[f])

    def edge_second(xi):
        ahead = [pltpu.roll(E2h[f], 126 - 6 * xi, 1) for f in range(FIELDS)]
        new = advance([edge_pair(H1, ahead, f, xi, 1) for f in range(FIELDS)], theta_main[1])
        for f in range(FIELDS):
            tile = ended(new[f], ahead[f])
            out[f, xi - 2, 0:2] = tile[1:3]
            out[f, xi - 2, 14:16] = tile[5:7]

    each(2, 18, 4, edge_second)

    for copy in corners + second + second_sides + [planes]:
        copy.wait_send()

    @pl.when(early)
    def _():
        @pl.when(middle)
        def _():
            on_up.wait_send()

        @pl.when(up_far)
        def _():
            up_r.wait_send()
            up_a.wait_send()

        @pl.when(down_far)
        def _():
            down_r.wait_send()
            down_a.wait_send()

    @pl.when(~up_far)
    def _():
        up_a.wait_send()
        up_b.wait_send()

    @pl.when(~down_far)
    def _():
        down_a.wait_send()
        down_b.wait_send()

    for copy in sides:
        copy.wait_send()


def shards(sizes, state, mobility, seeds, frame_shifts):
    V = pltpu.VMEM
    spec = pl.BlockSpec
    return pl.pallas_call(
        functools.partial(kernel, sizes),
        out_shape=jax.ShapeDtypeStruct(state.shape, f32),
        in_specs=[
            spec(memory_space=pltpu.SMEM),
            spec(memory_space=pltpu.SMEM),
            spec(memory_space=pl.ANY),
            spec(memory_space=pl.ANY),
        ],
        out_specs=spec(memory_space=pltpu.VMEM),
        scratch_shapes=[
            V((FIELDS, 20, 16, 128), f32),
            V((FIELDS, 20, 16, 128), f32),
            V((FIELDS, 20, 8, 128), f32),
            V((FIELDS, 20, 8, 128), f32),
            V((FIELDS, 8, 2, 128), f32),
            V((FIELDS + 2, 16, 128), f32),
            V((FIELDS + 2, 16, 128), f32),
            V((16, 128), f32),
            V((16, 128), f32),
            V((8, 128), f32),
            V((8, 128), f32),
            V((FIELDS, 8, 128), f32),
            V((FIELDS, 16, 128), f32),
            V((FIELDS, 8, 128), f32),
            V((FIELDS, 16, 128), f32),
            V((FIELDS, 8, 128), f32),
            V((FIELDS, 16, 128), f32),
            V((FIELDS, 8, 128), f32),
            V((24, 128), f32),
            V(seeds.shape, jnp.int32),
            pltpu.SemaphoreType.DMA((4,)),
            pltpu.SemaphoreType.DMA((20,)),
            pltpu.SemaphoreType.DMA((20,)),
            pltpu.SemaphoreType.REGULAR,
            pltpu.SemaphoreType.REGULAR,
        ],
        compiler_params=pltpu.CompilerParams(collective_id=0, has_side_effects=True),
    )(mobility, frame_shifts, state, seeds)


def solution(mesh):
    sizes = tuple(mesh.shape[a] for a in ("gx", "gy", "gz"))
    placed = (P(None, "gx", "gy", "gz"), P(), P(), P())
    return jax.shard_map(
        functools.partial(shards, sizes), mesh=mesh, in_specs=placed, out_specs=P(None, "gx", "gy", "gz"), check_vma=False
    )
```

```python
import functools

import jax
import jax.numpy as jnp
from jax import lax
from jax.experimental import pallas as pl
from jax.experimental.pallas import tpu as pltpu
from jax.sharding import PartitionSpec as P

step_rate = 0.1
stiffness = 0.7
coupling = 0.5
diffusion = 0.14
rejection = 0.5
nucleus = 0.3
melt_solute = 1.0

MESH = pl.DeviceIdType.MESH
FIELDS = 9
GRAINS = 8
W = 16
COLUMN = 4
f32 = jnp.float32


def iota(shape, dim):
    return lax.broadcasted_iota(jnp.int32, shape, dim)


def kernel(sizes, mob, shifts, state, seeds, out, F0, F1, H0, H1, relay, pack, packed, xl, xr, xlh, xrh, eh,
           E0m, E0h, E1m, E1h, E2m, E2h, marks, seedbuf, local, send, recv,
           far_ready, ring_ready):
    nx, ny, nz = sizes
    gx, gy, gz = lax.axis_index("gx"), lax.axis_index("gy"), lax.axis_index("gz")
    col = lax.rem(gy, COLUMN)

    def at(dx, dy, dz=0):
        return (lax.rem(gx + dx + nx, nx), lax.rem(gy + dy + ny, ny), lax.rem(gz + dz + nz, nz))

    early = gy < ny // 2
    far = at(0, jnp.where(col >= 2, 2, -2))
    around = [(1, 0), (-1, 0), (0, 1), (0, -1), (1, 1), (1, -1), (-1, 1), (-1, -1)]
    up_far, down_far = col == COLUMN - 1, col == 0
    middle = (col == 1) | (col == 2)

    def crosses(dy):
        return up_far if dy == 1 else down_far

    def even(dx):
        other = lax.rem(gx + dx + nx, nx)
        return (jnp.minimum(gx, other) >= nx // 2) & (jnp.maximum(gx, other) < nx - 1)

    barrier = pltpu.get_barrier_semaphore()

    def tell(semaphore, device):
        pl.semaphore_signal(semaphore, inc=1, device_id=device, device_id_type=MESH)

    for dz in (1, -1):
        tell(barrier, at(0, 0, dz))
    for dx, dy in around:
        silent = (gx == nx - 1) if dx == 1 else None
        if dy:
            cross = crosses(dy)
            held = cross & ~early & ~even(dx)
            if silent is not None:
                held = held | (~cross & silent)
        else:
            held = silent
        if held is None:
            tell(barrier, at(dx, dy))
        else:
            @pl.when(~held)
            def _(dx=dx, dy=dy):
                tell(barrier, at(dx, dy))

    @pl.when(early | even(0))
    def _():
        tell(barrier, far)

    own = [
        pltpu.make_async_copy(state, F0.at[:, 2:18], local.at[0]),
        pltpu.make_async_copy(state.at[:, :, 0:2], H0.at[:, 2:18, 2:4], local.at[1]),
        pltpu.make_async_copy(state.at[:, :, 14:16], H0.at[:, 2:18, 4:6], local.at[2]),
        pltpu.make_async_copy(seeds, seedbuf, local.at[3]),
    ]
    for copy in own:
        copy.start()

    lane = iota((8, 128), 1)
    row = iota((8, 128), 0)
    group = lane // 6
    spot = lane - 6 * group
    tiles = (slice(0, 8), slice(8, 16))
    halo = slice(16, 24)

    uneven = [jnp.where(even(dx), 0, 1) for dx in (-1, 0, 1)]
    n_far = jnp.where(middle, uneven[1], uneven[0] + 2 * uneven[1] + uneven[2])
    n_ring = jnp.where(middle, 3, 2)
    first_end, last_end = gx == 0, gx == nx - 1
    n_near = 11 - n_far - jnp.where(first_end | last_end, n_ring, 0)
    pl.semaphore_wait(barrier, n_near + jnp.where(early, 0, n_far) + jnp.where(last_end, n_ring, 0))

    @pl.when(~early)
    def _():
        @pl.when(~even(0))
        def _():
            tell(far_ready, far)

        for dy in (1, -1):
            for dx in (-1, 0, 1):
                @pl.when(crosses(dy) & ~even(dx))
                def _(dx=dx, dy=dy):
                    tell(far_ready, at(dx, dy))

    @pl.when(last_end)
    def _():
        tell(ring_ready, at(1, 0))
        for dy in (1, -1):
            @pl.when(~crosses(dy))
            def _(dy=dy):
                tell(ring_ready, at(1, dy))

    def remote(src, dst, s, r, device):
        return pltpu.make_async_remote_copy(
            src_ref=src, dst_ref=dst, send_sem=send.at[s], recv_sem=recv.at[r], device_id=device, device_id_type=MESH
        )

    A, B = slice(0, 8), slice(8, 16)
    hA, hB = slice(2, 10), slice(10, 18)
    top, bottom = slice(14, 16), slice(0, 2)
    up_a = remote(state.at[:, A, top], H0.at[:, hA, 0:2], 0, 0, at(0, 1))
    up_b = remote(state.at[:, B, top], H0.at[:, hB, 0:2], 1, 1, at(0, 1))
    down_a = remote(state.at[:, A, bottom], H0.at[:, hA, 6:8], 2, 2, at(0, -1))
    down_b = remote(state.at[:, B, bottom], H0.at[:, hB, 6:8], 3, 3, at(0, -1))
    up_r = remote(state.at[:, B, top], relay, 1, 4, at(0, -1))
    down_r = remote(state.at[:, B, bottom], relay, 3, 4, at(0, 1))
    on_up = remote(relay, H0.at[:, hB, 0:2], 4, 1, far)
    on_down = remote(relay, H0.at[:, hB, 6:8], 4, 3, far)
    sides = [
        remote(state.at[:, 14:16], F0.at[:, 0:2], 5, 5, at(1, 0)),
        remote(state.at[:, 0:2], F0.at[:, 18:20], 6, 6, at(-1, 0)),
    ]
    corners = [
        remote(state.at[:, 15:16, 15:16], H0.at[:, 1:2, 1:2], 7, 7, at(1, 1)),
        remote(state.at[:, 15:16, 0:1], H0.at[:, 1:2, 6:7], 8, 8, at(1, -1)),
        remote(state.at[:, 0:1, 15:16], H0.at[:, 18:19, 1:2], 9, 9, at(-1, 1)),
        remote(state.at[:, 0:1, 0:1], H0.at[:, 18:19, 6:7], 10, 10, at(-1, -1)),
    ]
    planes = remote(pack, packed, 11, 11, at(0, 0, -1))

    def begin(copies, when):
        for (dx, dy), copy in copies:
            cross = crosses(dy) if dy else jnp.bool_(False)
            waits_far = cross & early & ~even(dx)
            waits_ring = (first_end & ~cross) if dx == -1 else jnp.bool_(False)
            cond = [~waits_far & ~waits_ring, waits_ring, waits_far][when]

            @pl.when(cond)
            def _(copy=copy):
                copy.start()

    turns = [(1, 1), (1, -1), (-1, 1), (-1, -1)]
    corners_to = list(zip(turns, corners))
    sides_to = list(zip([(1, 0), (-1, 0)], sides))

    @pl.when(up_far)
    def _():
        up_r.start()

    @pl.when(down_far)
    def _():
        down_r.start()

    def send_far():
        @pl.when(up_far)
        def _():
            up_a.start()

        @pl.when(down_far)
        def _():
            down_a.start()

    soon = ~early | even(0)

    @pl.when(~early)
    def _():
        send_far()

    @pl.when(early)
    def _():
        begin(sides_to, 0)

    @pl.when(early & soon)
    def _():
        send_far()

    @pl.when(~up_far)
    def _():
        up_a.start()
        up_b.start()

    @pl.when(~down_far)
    def _():
        down_a.start()
        down_b.start()

    begin(corners_to, 0)

    own[0].wait()
    for f in range(FIELDS):
        for t in range(2):
            acc = jnp.zeros((8, 128), f32)
            for x in range(W):
                moved = pltpu.roll(F0[f, x + 2, tiles[t]], 6 * (x + 2) + 2, 1)
                acc = jnp.where((group == x + 2) & (spot >= 2), moved, acc)
            pack[f, tiles[t]] = acc
    for t in range(2):
        low = jnp.zeros((8, 128), f32)
        high = jnp.zeros((8, 128), f32)
        for f in range(FIELDS):
            acc = pack[f, tiles[t]]
            here = lane // 12 == f
            low = jnp.where(here, pltpu.roll(acc, (12 * f - 12) % 128, 1), low)
            high = jnp.where(here, pltpu.roll(acc, (12 * f - 96) % 128, 1), high)
        pack[FIELDS, tiles[t]] = low
        pack[FIELDS + 1, tiles[t]] = high

    own[3].wait()
    first_moves = jnp.full((8, 128), shifts[0], jnp.int32) == 2
    first_rows = jnp.full((256, 128), shifts[0], jnp.int32) == 2
    r24 = iota((24, 128), 0)
    offset = jnp.where(r24 < 16, r24, jnp.where(r24 < 20, r24 - 18, r24 - 6))
    wanted = lax.rem(gy * W + offset + ny * W, ny * W)
    pick = (iota((24, 128), 1) == wanted).astype(f32)
    xrow = iota((256, 128), 0)
    wlane = iota((256, 128), 1)
    wgroup = wlane // 6
    wspot = wlane - 6 * wgroup
    same = lax.rem(gx * W - 2 + wgroup + nx * W, nx * W) == xrow
    total = jnp.zeros((24, 128), f32)
    for k in range(2):
        grid = jnp.where(first_rows, seedbuf[0, k], seedbuf[1, k]).astype(f32)
        lines = lax.dot_general(pick, grid, (((1,), (1,)), ((), ())), preferred_element_type=f32)
        spread = (same & (wspot == 2 + k)).astype(f32)
        total = total + jnp.dot(lines, spread, preferred_element_type=f32)
    marks[...] = total

    planes.start()

    def pass_on():
        @pl.when(col == 2)
        def _():
            up_r.wait_recv()
            on_up.start()

        @pl.when(col == 1)
        def _():
            down_r.wait_recv()
            on_down.start()

    @pl.when(soon)
    def _():
        pass_on()

    planes.wait_recv()
    second = [
        remote(packed.at[0:FIELDS, top], eh.at[:, 0:2], 12, 12, at(0, 1)),
        remote(packed.at[0:FIELDS, bottom], eh.at[:, 6:8], 13, 13, at(0, -1)),
        remote(packed.at[FIELDS + 1, 15:16], xlh.at[1:2], 16, 16, at(1, 1)),
        remote(packed.at[FIELDS + 1, 0:1], xlh.at[6:7], 17, 17, at(1, -1)),
        remote(packed.at[FIELDS, 15:16], xrh.at[1:2], 18, 18, at(-1, 1)),
        remote(packed.at[FIELDS, 0:1], xrh.at[6:7], 19, 19, at(-1, -1)),
    ]
    second_sides = [
        remote(packed.at[FIELDS + 1], xl, 14, 14, at(1, 0)),
        remote(packed.at[FIELDS], xr, 15, 15, at(-1, 0)),
    ]
    second_to = list(zip([(0, 1), (0, -1)] + turns, second)) + list(zip([(1, 0), (-1, 0)], second_sides))
    begin(second_to, 0)

    last = jnp.full((8, 128), gz, jnp.int32) == nz - 1
    lowest = jnp.full((8, 128), gz, jnp.int32) == 0
    enters = (spot == 2) | (spot == 3)
    final = lane == 127

    rates = [step_rate * mob[g] for g in range(GRAINS)]
    keep = [1.0 - 6.0 * stiffness * r for r in rates]
    spreadrate = [stiffness * r for r in rates]

    def advance(pairs, theta):
        c = [p[0] for p in pairs]
        beside = [p[1] for p in pairs]
        squares = c[0] * c[0]
        for g in range(1, GRAINS):
            squares = squares + c[g] * c[g]
        s = c[GRAINS]
        well = squares - theta + coupling * s
        fresh = []
        after = None
        for g in range(GRAINS):
            new = c[g] * (keep[g] - rates[g] * well) + spreadrate[g] * beside[g]
            after = new * new if after is None else after + new * new
            fresh.append(new)
        solute = s * ((1.0 - 6.0 * diffusion) - rejection * (after - squares)) + diffusion * beside[GRAINS]
        return fresh + [solute]

    def theta_of(plane):
        return 1.0 - 2.0 * (plane.astype(f32) + 0.5) / (nz * 128.0)

    base_plane = gz * 128
    shift1 = jnp.full((8, 128), shifts[0], jnp.int32)
    theta_main = [theta_of(base_plane + lane - shift1), theta_of(base_plane + lane - 2)]
    theta_pack = [theta_of(base_plane + 126 + spot - shift1), theta_of(base_plane + 126 + spot - 2)]
    open_below = [~(lowest & first_moves & (lane == 2)), ~(lowest & (lane == 2))]

    def entering(f, rows):
        if f == GRAINS:
            return jnp.full((8, 128), melt_solute, f32)
        return jnp.where(marks[rows] == float(f), nucleus, 0.0)

    def at_top(tile, f, rows):
        edge = jnp.where(first_moves & enters, entering(f, rows), 0.0)
        return jnp.where(last & (spot >= 2), edge, tile)

    def settle(new, f, rows):
        edge = jnp.where(enters, jnp.where(first_moves, new, entering(f, rows)), 0.0)
        return jnp.where(last & (spot >= 2), edge, new)

    def own_planes(acc, tile, xi):
        return jnp.where((group == xi) & (spot < 2), pltpu.roll(tile, (6 * xi + 2) % 128, 1), acc)

    def side_planes(tile, left, right, f):
        tile = jnp.where(lane < 12, pltpu.roll(left, (-12 * f) % 128, 1), tile)
        return jnp.where((lane >= 108) & (lane < 120), pltpu.roll(right, (108 - 12 * f) % 128, 1), tile)

    def rows_beside(F, index, t, f):
        tile = F[index + (tiles[t],)]
        other = F[index + (tiles[1 - t],)]
        if t == 0:
            return tile, pltpu.roll(tile, 1, 0) + jnp.where(row == 7, pltpu.roll(other, 7, 0), pltpu.roll(tile, 7, 0))
        return tile, jnp.where(row == 0, pltpu.roll(other, 1, 0), pltpu.roll(tile, 1, 0)) + pltpu.roll(tile, 7, 0)

    def planes_beside(tile, nextplane, step):
        below = jnp.where(open_below[step], pltpu.roll(tile, 1, 1), 0.0)
        return below + jnp.where(final, nextplane, pltpu.roll(tile, 127, 1))

    def lanes_beside(tile):
        return pltpu.roll(tile, 6, 1) + pltpu.roll(tile, 122, 1) + pltpu.roll(tile, 1, 1) + pltpu.roll(tile, 127, 1)

    def main_pair(F, ahead, f, xi, t, step):
        tile, beside = rows_beside(F, (f, xi), t, f)
        beside = beside + F[f, xi - 1, tiles[t]] + F[f, xi + 1, tiles[t]]
        return tile, beside + planes_beside(tile, ahead[f], step)

    def pack_pair(E, f, t):
        tile, beside = rows_beside(E, (f,), t, f)
        return tile, beside + lanes_beside(tile)

    def edge_pair(H, ahead, f, xi, step):
        tile = H[f, xi]
        beside = pltpu.roll(tile, 1, 0) + pltpu.roll(tile, 7, 0) + H[f, xi - 1] + H[f, xi + 1]
        return tile, beside + planes_beside(tile, ahead[f], step)

    def edge_pack_pair(E, f):
        tile = E[f]
        return tile, pltpu.roll(tile, 1, 0) + pltpu.roll(tile, 7, 0) + lanes_beside(tile)

    def pack_steps(which):
        for t in range(2):
            if which == 1:
                new = advance([pack_pair(E0m, f, t) for f in range(FIELDS)], theta_pack[0])
                for f in range(FIELDS):
                    E1m[f, tiles[t]] = settle(new[f], f, tiles[t])
            else:
                new = advance([pack_pair(E1m, f, t) for f in range(FIELDS)], theta_pack[1])
                for f in range(FIELDS):
                    E2m[f, tiles[t]] = joined(E1m[f, tiles[t]], new[f])

    def main_first(xi):
        for t in range(2):
            ahead = [pltpu.roll(E0m[f, tiles[t]], 125 - 6 * xi, 1) for f in range(FIELDS)]
            new = advance([main_pair(F0, ahead, f, xi, t, 0) for f in range(FIELDS)], theta_main[0])
            for f in range(FIELDS):
                F1[f, xi, tiles[t]] = new[f]

    def joined(first, second):
        return jnp.where(spot == 1, pltpu.roll(first, 127, 1), second)

    def ended(new, ahead):
        return pltpu.roll(jnp.where(lane < 2, ahead, new), 126, 1)

    def main_second(xi):
        for t in range(2):
            ahead = [pltpu.roll(E2m[f, tiles[t]], 126 - 6 * xi, 1) for f in range(FIELDS)]
            new = advance([main_pair(F1, ahead, f, xi, t, 1) for f in range(FIELDS)], theta_main[1])
            for f in range(FIELDS):
                out[f, xi - 2, tiles[t]] = ended(new[f], ahead[f])

    def each(lo, hi, unroll, step):
        def body(i, carry):
            step(i)
            return carry

        lax.fori_loop(lo, hi, body, 0, unroll=unroll)

    for f in range(FIELDS):
        for t in range(2):
            tile = at_top(packed[f, tiles[t]], f, tiles[t])
            for xi in range(2, 18):
                tile = own_planes(tile, F0[f, xi, tiles[t]], xi)
            E0m[f, tiles[t]] = tile
    pack_steps(1)
    pack_steps(2)
    each(3, 17, 2, main_first)
    each(4, 16, 2, main_second)

    @pl.when(~early)
    def _():
        @pl.when(up_far)
        def _():
            up_r.wait_send()
            up_a.wait_send()

        @pl.when(down_far)
        def _():
            down_r.wait_send()
            down_a.wait_send()

        @pl.when(middle)
        def _():
            on_up.wait_send()

        begin(sides_to, 0)

    @pl.when(first_end)
    def _():
        pl.semaphore_wait(ring_ready, n_ring)
        begin(sides_to, 1)
        begin(corners_to, 1)
        begin(second_to, 1)

    @pl.when(early)
    def _():
        @pl.when(n_far > 0)
        def _():
            pl.semaphore_wait(far_ready, n_far)

        @pl.when(~soon)
        def _():
            send_far()

        begin(corners_to, 2)
        begin(second_to, 2)

        @pl.when(~soon)
        def _():
            pass_on()

    for copy in own[1:3]:
        copy.wait()
    for copy in sides + second_sides:
        copy.wait_recv()
    trims = [
        pltpu.make_async_copy(F0.at[:, lo:lo + 2, y:y + 2], H0.at[:, lo:lo + 2, r:r + 2], local.at[i])
        for i, (lo, y, r) in enumerate([(0, 0, 2), (0, 14, 4), (18, 0, 2), (18, 14, 4)])
    ]
    for copy in trims:
        copy.start()
    for f in range(FIELDS):
        for t in range(2):
            tile = side_planes(E0m[f, tiles[t]], xl[tiles[t]], xr[tiles[t]], f)
            tile = at_top(tile, f, tiles[t])
            for xi in (0, 1, 18, 19):
                tile = own_planes(tile, F0[f, xi, tiles[t]], xi)
            E0m[f, tiles[t]] = tile
    pack_steps(1)
    pack_steps(2)
    for xi in (1, 2, 17, 18):
        main_first(xi)
    for xi in (2, 3, 16, 17):
        main_second(xi)
    for copy in trims:
        copy.wait()

    for copy in corners + second:
        copy.wait_recv()
    up_a.wait_recv()
    down_a.wait_recv()
    up_b.wait_recv()
    down_b.wait_recv()

    inner = (row >= 2) & (row < 6)
    for f in range(FIELDS):
        tile = side_planes(eh[f], xlh[...], xrh[...], f)
        tile = at_top(tile, f, halo)
        mid = jnp.where(row < 4, pltpu.roll(E0m[f, 0:8], 2, 0), pltpu.roll(E0m[f, 8:16], 6, 0))
        for xi in range(1, 19):
            tile = own_planes(tile, H0[f, xi], xi)
        E0h[f] = jnp.where(inner, mid, tile)

    def between(new, t0, t1):
        first = jnp.where(row < 2, pltpu.roll(new, 7, 0), pltpu.roll(t0, 1, 0))
        second = jnp.where(row < 6, pltpu.roll(t1, 7, 0), pltpu.roll(new, 1, 0))
        return jnp.where(row < 4, first, second)

    new = advance([edge_pack_pair(E0h, f) for f in range(FIELDS)], theta_pack[0])
    for f in range(FIELDS):
        E1h[f] = between(settle(new[f], f, halo), E1m[f, 0:8], E1m[f, 8:16])

    def edge_first(xi):
        ahead = [pltpu.roll(E0h[f], 125 - 6 * xi, 1) for f in range(FIELDS)]
        new = advance([edge_pair(H0, ahead, f, xi, 0) for f in range(FIELDS)], theta_main[0])
        for f in range(FIELDS):
            H1[f, xi] = between(new[f], F1[f, xi, 0:8], F1[f, xi, 8:16])

    each(1, 19, 3, edge_first)
    new = advance([edge_pack_pair(E1h, f) for f in range(FIELDS)], theta_pack[1])
    for f in range(FIELDS):
        E2h[f] = joined(E1h[f], new[f])

    def edge_second(xi):
        ahead = [pltpu.roll(E2h[f], 126 - 6 * xi, 1) for f in range(FIELDS)]
        new = advance([edge_pair(H1, ahead, f, xi, 1) for f in range(FIELDS)], theta_main[1])
        for f in range(FIELDS):
            tile = ended(new[f], ahead[f])
            out[f, xi - 2, 0:2] = tile[1:3]
            out[f, xi - 2, 14:16] = tile[5:7]

    each(2, 18, 4, edge_second)

    for copy in corners + second + second_sides + [planes]:
        copy.wait_send()

    @pl.when(early)
    def _():
        @pl.when(middle)
        def _():
            on_up.wait_send()

        @pl.when(up_far)
        def _():
            up_r.wait_send()
            up_a.wait_send()

        @pl.when(down_far)
        def _():
            down_r.wait_send()
            down_a.wait_send()

    @pl.when(~up_far)
    def _():
        up_a.wait_send()
        up_b.wait_send()

    @pl.when(~down_far)
    def _():
        down_a.wait_send()
        down_b.wait_send()

    for copy in sides:
        copy.wait_send()


def shards(sizes, state, mobility, seeds, frame_shifts):
    V = pltpu.VMEM
    spec = pl.BlockSpec
    return pl.pallas_call(
        functools.partial(kernel, sizes),
        out_shape=jax.ShapeDtypeStruct(state.shape, f32),
        in_specs=[
            spec(memory_space=pltpu.SMEM),
            spec(memory_space=pltpu.SMEM),
            spec(memory_space=pl.ANY),
            spec(memory_space=pl.ANY),
        ],
        out_specs=spec(memory_space=pltpu.VMEM),
        scratch_shapes=[
            V((FIELDS, 20, 16, 128), f32),
            V((FIELDS, 20, 16, 128), f32),
            V((FIELDS, 20, 8, 128), f32),
            V((FIELDS, 20, 8, 128), f32),
            V((FIELDS, 8, 2, 128), f32),
            V((FIELDS + 2, 16, 128), f32),
            V((FIELDS + 2, 16, 128), f32),
            V((16, 128), f32),
            V((16, 128), f32),
            V((8, 128), f32),
            V((8, 128), f32),
            V((FIELDS, 8, 128), f32),
            V((FIELDS, 16, 128), f32),
            V((FIELDS, 8, 128), f32),
            V((FIELDS, 16, 128), f32),
            V((FIELDS, 8, 128), f32),
            V((FIELDS, 16, 128), f32),
            V((FIELDS, 8, 128), f32),
            V((24, 128), f32),
            V(seeds.shape, jnp.int32),
            pltpu.SemaphoreType.DMA((4,)),
            pltpu.SemaphoreType.DMA((20,)),
            pltpu.SemaphoreType.DMA((20,)),
            pltpu.SemaphoreType.REGULAR,
            pltpu.SemaphoreType.REGULAR,
        ],
        compiler_params=pltpu.CompilerParams(collective_id=0, has_side_effects=True),
    )(mobility, frame_shifts, state, seeds)


def solution(mesh):
    sizes = tuple(mesh.shape[a] for a in ("gx", "gy", "gz"))
    placed = (P(None, "gx", "gy", "gz"), P(), P(), P())
    return jax.shard_map(
        functools.partial(shards, sizes), mesh=mesh, in_specs=placed, out_specs=P(None, "gx", "gy", "gz"), check_vma=False
    )
```
